32 devices in a mesh: dp: 2 (over x), fsdp: 16 (over z, y, core).
Axes of the slice: x: 2, y: 2, z: 4, core: 2. Of those that a mesh axis runs over, the one named last changes fastest.
Arguments:
- tokens: bfloat16 [32, 256, 1024], P(('dp', 'fsdp')), may hold values from -6 to 6
- segment_ids: int32 [32, 256], P(('dp', 'fsdp')), may hold values from 0 to 3, never falling along the last dimension, each value on 1 to 128 neighbouring positions
- cotangent: bfloat16 [32, 256, 1024], P(('dp', 'fsdp')), may hold values from -6 to 6
- ln_gain: bfloat16 [2, 1024], P(None, ('dp', 'fsdp')), may hold values from 0.5 to 1.5
- ln_bias: bfloat16 [2, 1024], P(None, ('dp', 'fsdp')), may hold values from -1.75 to 1.75
- w_qkv: bfloat16 [2, 1024, 3072], P(None, ('dp', 'fsdp')), may hold values from -0.1875 to 0.1875
- w_out: bfloat16 [2, 1024, 1024], P(None, ('dp', 'fsdp')), may hold values from -0.75 to 0.75
- w_in: bfloat16 [2, 1024, 4096], P(None, ('dp', 'fsdp')), may hold values from -0.1875 to 0.1875
- b_in: bfloat16 [2, 4096], P(None, ('dp', 'fsdp')), may hold values from -3 to 3
- w_fo: bfloat16 [2, 4096, 1024], P(None, ('dp', 'fsdp')), may hold values from -0.125 to 0.125
- b_fo: bfloat16 [2, 1024], P(None, ('dp', 'fsdp')), may hold values from -1.75 to 1.75
Outputs:
- layer_out: bfloat16 [32, 256, 1024], P(('dp', 'fsdp'))
- d_tokens: float32 [32, 256, 1024], P(('dp', 'fsdp'))
- d_ln_gain: float32 [2, 1024], P(None, ('dp', 'fsdp'))
- d_ln_bias: float32 [2, 1024], P(None, ('dp', 'fsdp'))
- d_w_qkv: float32 [2, 1024, 3072], P(None, ('dp', 'fsdp'))
- d_w_out: float32 [2, 1024, 1024], P(None, ('dp', 'fsdp'))
- d_w_in: float32 [2, 1024, 4096], P(None, ('dp', 'fsdp'))
- d_b_in: float32 [2, 4096], P(None, ('dp', 'fsdp'))
- d_w_fo: float32 [2, 4096, 1024], P(None, ('dp', 'fsdp'))
- d_b_fo: float32 [2, 1024], P(None, ('dp', 'fsdp'))
The draws below stay inside these ranges and needn't reach their ends.
Inputs may be any that keep to these rules, and one draw needn't show every extreme that they name: `segment_ids`: in each row of 256 tokens the protein ids never fall; each of the 4 proteins has 1 to 128 tokens.
All inputs are finite; a program needn't handle non-finite values.
Results may differ from the reference program's by a relative error of at most 0.013.
Values may be sent and summed in bfloat16 or wider, within the bound.
No kernel may reach another device: no remote copies, remote signals or barrier semaphores. Data moves between devices by JAX's collectives and lax.ppermute only.
A program may use at most 320 MiB of HBM per device.

```python
import math
import jax
import jax.numpy as jnp
import numpy as np
from jax import lax

D = 1024
HEADS = 16
HEAD = 64
ROT = 32
FF = 4096
LAYERS = 2
SEQ = 256
PROT = 4
LONGEST = 128
SEQS = 32


def with_spikes(values, key, source, target, shards_of, factor):
    owner, partner = [(jnp.arange(values.shape[axis_at]) // (values.shape[axis_at] // shards_of)).reshape([-1 if axis == axis_at else 1 for axis in range(values.ndim)]) for axis_at in (source, target)]
    chosen = jax.random.permutation(key, shards_of)[partner]
    strong = (owner == chosen) | (owner == (partner + shards_of // 2) % shards_of)
    return jnp.where(strong, factor * values, values)


def shard_levels(key, dims, cuts, low, largest):
    level, own = 1.0, jax.random.fold_in(key, 6)
    for axis_at, shards_of in cuts:
        heights = jnp.exp(jax.random.uniform(jax.random.fold_in(own, axis_at), (shards_of,), jnp.float32, low / len(cuts), largest / len(cuts)))
        level = level * jnp.repeat(heights, dims[axis_at] // shards_of).reshape([-1 if axis == axis_at else 1 for axis in range(len(dims))])
    return level


def length_profile(amount, total, bound, lean):
    loads = [(1 << 20) // math.isqrt(standing ** lean) + 1 for standing in range(2, amount + 1)]
    spare, holding = total - bound - (amount - 1), [1] * (amount - 1)
    while spare > 0:
        movable = [i for i in range(amount - 1) if holding[i] < bound]
        mass, budget = sum([loads[i] for i in movable]), spare
        for i in movable:
            addition = min(bound - holding[i], max(1, budget * loads[i] // mass), spare)
            holding[i] = holding[i] + addition
            spare = spare - addition
    return np.array([bound] + holding)


def uneven_parts(rng, number_of, total, limit, skew):
    if number_of == 2:
        one = jax.random.randint(rng, (), max(1, total - limit), min(limit, total - 1) + 1)
        return jnp.stack([one, total - one])
    sizes = jnp.asarray(length_profile(number_of, total, limit, skew), jnp.int32)
    couples = (number_of - 1) // 2
    giver, taker = sizes[1:1 + 2 * couples:2], sizes[2:2 + 2 * couples:2]
    room = jnp.minimum(giver - 1, limit - taker)
    shifted = jax.random.randint(jax.random.fold_in(rng, 1), (couples,), 0, 1 << 20) % (room + 1)
    sizes = sizes.at[1:1 + 2 * couples:2].set(giver - shifted).at[2:2 + 2 * couples:2].set(taker + shifted)
    return sizes[jax.random.permutation(jax.random.fold_in(rng, 2), number_of)]


def bell_draw(rng, shape, spread, most, shards=(), kind=jnp.bfloat16):
    entries = spread * jax.random.normal(rng, shape, jnp.float32)
    if shards:
        entries = entries * shard_levels(rng, shape, shards, -0.22, 0.18)
    return jnp.clip(entries, -most, most).astype(kind)


def bell_draw_with(rng, shape, deviation, limit, shards, heavy, kind=jnp.bfloat16):
    entries = deviation * jax.random.normal(rng, shape, jnp.float32)
    if shards:
        entries = entries * shard_levels(rng, shape, shards, -0.22, 0.18)
    return jnp.clip(with_spikes(entries, jax.random.fold_in(rng, 3), *heavy), -limit, limit).astype(kind)


def setup_inputs(seed: int = 0) -> dict:
    seeds = jax.random.split(jax.random.key(seed), 12)
    tokens = bell_draw(seeds[0], (SEQS, SEQ, D), 1.0, 6.0, ((0, 32),))
    segment_ids = jax.vmap(lambda own: jnp.searchsorted(jnp.cumsum(uneven_parts(own, PROT, SEQ, LONGEST, 2)), jnp.arange(SEQ), side="right"))(jax.random.split(seeds[1], SEQS)).reshape((SEQS, SEQ)).astype(jnp.int32)
    cotangent = bell_draw_with(seeds[2], (SEQS, SEQ, D), 1.0, 6.0, ((0, 32),), (0, 2, 32, 2.75))
    ln_gain = jnp.clip(1.0 + 0.1 * jax.random.normal(seeds[3], (LAYERS, D), jnp.float32), 0.5, 1.5).astype(jnp.bfloat16)
    ln_bias = bell_draw(seeds[4], (LAYERS, D), 0.3, 1.75, ((1, 32),))
    w_qkv = bell_draw(seeds[5], (LAYERS, D, 3 * D), D ** -0.5, 0.1875, ((1, 32),))
    w_out = bell_draw(seeds[6], (LAYERS, D, D), (D // 16) ** -0.5, 0.75, ((1, 32),))
    w_in = bell_draw(seeds[7], (LAYERS, D, FF), D ** -0.5, 0.1875, ((1, 32),))
    b_in = bell_draw(seeds[8], (LAYERS, FF), 0.5, 3.0, ((1, 32),))
    w_fo = bell_draw(seeds[9], (LAYERS, FF, D), (FF // 2) ** -0.5, 0.125, ((1, 32),))
    b_fo = bell_draw(seeds[10], (LAYERS, D), 0.3, 1.75, ((1, 32),))
    return {"tokens": tokens, "segment_ids": segment_ids, "cotangent": cotangent, "ln_gain": ln_gain, "ln_bias": ln_bias, "w_qkv": w_qkv, "w_out": w_out, "w_in": w_in, "b_in": b_in, "w_fo": w_fo, "b_fo": b_fo}


@jax.custom_vjp
def low(v):
    return lax.optimization_barrier(v.astype(jnp.bfloat16)).astype(jnp.float32)

@jax.custom_vjp
def low_back(v):
    return v

def low_keep(v):
    return (low(v), None)

def low_pass(kept, grad):
    return (grad,)

def back_keep(v):
    return (v, None)

def back_low(kept, grad):
    return (low(grad),)
low.defvjp(low_keep, low_pass)
low_back.defvjp(back_keep, back_low)
layer_eps = 1e-05
gelu_scale = 0.7978845608028654
masked_fill = -1000000000.0

def gelu_tanh(values):
    return 0.5 * values * (1.0 + jnp.tanh(gelu_scale * (values + 0.044715 * values * values * values)))

def positions_of(segment_ids):
    last_axis = segment_ids.ndim - 1
    index_grid = lax.broadcasted_iota(jnp.int32, segment_ids.shape, last_axis)
    earlier = jnp.concatenate([segment_ids[..., :1] - 1, segment_ids[..., :-1]], axis=last_axis)
    starts = jnp.where(segment_ids != earlier, index_grid, jnp.zeros_like(index_grid))
    starts = lax.cummax(starts, axis=last_axis)
    return index_grid - starts

def attention_mask(segment_ids):
    length = segment_ids.shape[-1]
    row_index = lax.broadcasted_iota(jnp.int32, (length, length), 0)
    col_index = lax.broadcasted_iota(jnp.int32, (length, length), 1)
    same_doc = segment_ids[:, :, None] == segment_ids[:, None, :]
    return jnp.logical_and(same_doc, (col_index <= row_index)[None])

def rotary_tables(positions, rot_dim):
    half_rot = rot_dim // 2
    frequency = 10000.0 ** (-(jnp.arange(half_rot, dtype=jnp.float32) * 2.0 / rot_dim))
    angles = positions.astype(jnp.float32)[..., None] * frequency
    return (jnp.cos(angles), jnp.sin(angles))

def rotate(values, cosine, sine_table, rot_dim):
    half_rot = rot_dim // 2
    leading = values[..., :half_rot]
    trailing = values[..., half_rot:rot_dim]
    cos_heads = cosine[..., None, :]
    sin_heads = sine_table[..., None, :]
    return jnp.concatenate([leading * cos_heads - trailing * sin_heads, trailing * cos_heads + leading * sin_heads, values[..., rot_dim:]], axis=-1)

def layer_norm(hidden, norm_gain, norm_shift):
    mean_value = lax.optimization_barrier(jnp.mean(hidden, axis=-1, keepdims=True))
    centered = hidden - mean_value
    variance = lax.optimization_barrier(jnp.mean(centered * centered, axis=-1, keepdims=True))
    return centered * lax.rsqrt(variance + layer_eps) * norm_gain + norm_shift

def block_forward(hidden, segment_ids, params):
    highest = lax.Precision.HIGHEST
    groups, length = segment_ids.shape
    positions = positions_of(segment_ids)
    cosine, sine_table = rotary_tables(positions, ROT)
    allowed = attention_mask(segment_ids)[:, None]
    score_scale = 1.0 / math.sqrt(HEAD)
    heads_shape = (groups, length, HEADS, HEAD)
    for depth in range(LAYERS):
        norm_gain, norm_shift, wq_all, wo_all, wi_all, bi_all, wf_all, bf_all = [item[depth] for item in params]
        normed = low(layer_norm(hidden, norm_gain, norm_shift))
        projected = low_back(jnp.einsum('gsd,de->gse', normed, wq_all, precision=highest))
        query_rows = projected[..., :D].reshape(heads_shape)
        key_rows = projected[..., D:2 * D].reshape(heads_shape)
        value_rows = projected[..., 2 * D:].reshape(heads_shape)
        rot_query = low(rotate(query_rows, cosine, sine_table, ROT))
        rot_key = low(rotate(key_rows, cosine, sine_table, ROT))
        value_low = low(value_rows)
        scores = low_back(jnp.einsum('gshe,gthe->ghst', rot_query, rot_key, precision=highest) * score_scale)
        scores = jnp.where(allowed, scores, masked_fill)
        weights_attn = low(jax.nn.softmax(scores, axis=-1))
        attended = jnp.einsum('ghst,gthe->gshe', weights_attn, value_low, precision=highest).reshape(groups, length, D)
        attended = low(low_back(attended))
        branch = low_back(jnp.einsum('gsd,de->gse', attended, wo_all, precision=highest))
        pre_act = low_back(jnp.einsum('gsd,df->gsf', normed, wi_all, precision=highest) + bi_all)
        activation = low(gelu_tanh(pre_act))
        mlp_out = low_back(jnp.einsum('gsf,fd->gsd', activation, wf_all, precision=highest) + bf_all)
        hidden = hidden + branch + mlp_out
    return hidden

def reference(tokens, segment_ids, cotangent, ln_gain, ln_bias, w_qkv, w_out, w_in, b_in, w_fo, b_fo):
    params = tuple((item.astype(jnp.float32) for item in (ln_gain, ln_bias, w_qkv, w_out, w_in, b_in, w_fo, b_fo)))
    group_size = math.gcd(SEQS, max(1, 4096 // SEQ))
    block_count = SEQS // group_size
    inputs = tokens.astype(jnp.float32).reshape(block_count, group_size, SEQ, D)
    seg_blocks = segment_ids.reshape(block_count, group_size, SEQ)
    checked = jax.checkpoint(block_forward)

    def network(inputs_all, weights):

        def advance(carry, block):
            return (carry, checked(block[0], block[1], weights))
        unused, result = lax.scan(advance, jnp.zeros((), jnp.float32), (inputs_all, seg_blocks))
        return result
    result, pullback = jax.vjp(network, inputs, params)
    d_inputs, d_params = pullback(cotangent.astype(jnp.float32).reshape(block_count, group_size, SEQ, D))
    return (result.reshape(SEQS, SEQ, D).astype(jnp.bfloat16), d_inputs.reshape(SEQS, SEQ, D), d_params[0], d_params[1], d_params[2], d_params[3], d_params[4], d_params[5], d_params[6], d_params[7])
```

```python
import jax
import jax.numpy as jnp
from jax import lax
from jax.sharding import PartitionSpec as P

HEADS = 16
HEAD = 64
ROT = 32
LAYERS = 2
AXES = ("dp", "fsdp")

CORE_BIT = 0
PAIR_BIT = 2
FIRST_BIT = 3

layer_eps = 1e-05
gelu_scale = 0.7978845608028654
masked_fill = -1000000000.0
f32 = jnp.float32
bf16 = jnp.bfloat16


def gelu_tanh(values):
    return (
        0.5 * values * (1.0 + jnp.tanh(gelu_scale * (values + 0.044715 * values * values * values)))
    )


def gelu_slope(values):
    inner = jnp.tanh(gelu_scale * (values + 0.044715 * values * values * values))
    return 0.5 * (1.0 + inner) + 0.5 * values * (1.0 - inner * inner) * gelu_scale * (
        1.0 + 3.0 * 0.044715 * values * values
    )


def positions_of(segment_ids):
    last_axis = segment_ids.ndim - 1
    index_grid = lax.broadcasted_iota(jnp.int32, segment_ids.shape, last_axis)
    earlier = jnp.concatenate([segment_ids[..., :1] - 1, segment_ids[..., :-1]], axis=last_axis)
    starts = jnp.where(segment_ids != earlier, index_grid, jnp.zeros_like(index_grid))
    starts = lax.cummax(starts, axis=last_axis)
    return index_grid - starts


def attention_mask(segment_ids):
    length = segment_ids.shape[-1]
    row_index = lax.broadcasted_iota(jnp.int32, (length, length), 0)
    col_index = lax.broadcasted_iota(jnp.int32, (length, length), 1)
    same_doc = segment_ids[:, :, None] == segment_ids[:, None, :]
    return jnp.logical_and(same_doc, (col_index <= row_index)[None])


def rotary_tables(positions, rot_dim):
    half_rot = rot_dim // 2
    frequency = 10000.0 ** (-(jnp.arange(half_rot, dtype=jnp.float32) * 2.0 / rot_dim))
    angles = positions.astype(jnp.float32)[..., None] * frequency
    return (jnp.cos(angles), jnp.sin(angles))


def rotate(values, cosine, sine_table, rot_dim):
    half_rot = rot_dim // 2
    leading = values[..., :half_rot]
    trailing = values[..., half_rot:rot_dim]
    cos_heads = cosine[..., None, :]
    sin_heads = sine_table[..., None, :]
    return jnp.concatenate(
        [
            leading * cos_heads - trailing * sin_heads,
            trailing * cos_heads + leading * sin_heads,
            values[..., rot_dim:],
        ],
        axis=-1,
    )


def norm_stats(hidden):
    mean_value = jnp.mean(hidden, axis=-1, keepdims=True)
    centered = hidden - mean_value
    variance = jnp.mean(centered * centered, axis=-1, keepdims=True)
    scale = lax.rsqrt(variance + layer_eps)
    return centered * scale, scale


def build(mesh):
    count = mesh.shape["dp"] * mesh.shape["fsdp"]
    bits = count.bit_length() - 1
    head_bits = HEADS.bit_length() - 1
    every = list(range(bits - 1, -1, -1))
    shared = [b for b in every if b not in (CORE_BIT, PAIR_BIT)]
    others = [b for b in shared if b != FIRST_BIT]
    deep_order = [FIRST_BIT] + others[::-1]
    wide_order = [FIRST_BIT] + others
    unit_bits = wide_order[::-1]
    stands = list(range(bits))
    for share_bit, head_bit in ((PAIR_BIT, 1), (CORE_BIT, 3)):
        target = bits - head_bits + head_bit
        if target != share_bit:
            stands[share_bit], stands[target] = target, share_bit
    exchange = [
        (i, sum(((i >> stands[b]) & 1) << b for b in range(bits))) for i in range(count)
    ]
    head_order = [stands[b] for b in every if stands[b] not in (CORE_BIT, PAIR_BIT)]

    def program(
        tokens, segment_ids, cotangent, ln_gain, ln_bias, w_qkv, w_out, w_in, b_in, w_fo, b_fo
    ):
        device = lax.axis_index(AXES)
        seq_len, width = tokens.shape[1:]
        rows = w_qkv.shape[1]
        units = w_fo.shape[1]
        share_units = units * count // 4
        share_width = width // 4

        def bit(b):
            return ((device >> b) & 1) == 1

        def cross(value, b):
            return lax.ppermute(value, AXES, [(i, i ^ (1 << b)) for i in range(count)])

        def pair_up(mine, other, b):
            flag = bit(b)
            return jnp.stack([jnp.where(flag, other, mine), jnp.where(flag, mine, other)])

        def gather(value, order):
            for b in order:
                value = pair_up(value, cross(value, b), b)
            return value

        def arrange(value, have, want):
            rest = list(range(len(have), value.ndim))
            return value.transpose([have.index(b) for b in want] + rest)

        def half(value, axis, own, b):
            flag = bit(b)
            low = lax.index_in_dim(value, 0, axis, keepdims=False)
            high = lax.index_in_dim(value, 1, axis, keepdims=False)
            return jnp.where(flag, high, low) if own else jnp.where(flag, low, high)

        def fold(value, axis, b):
            arrived = cross(half(value, axis, False, b).astype(bf16), b)
            return half(value, axis, True, b).astype(f32) + arrived.astype(f32)

        def spread(value):
            pair = jnp.stack([value, cross(value, PAIR_BIT)])
            return jnp.concatenate([pair, cross(pair, CORE_BIT)]).reshape(-1, value.shape[-1])

        def collect(partial):
            parts = partial.reshape(2, 2, seq_len, width)
            kept = parts[0] + cross(parts[1].astype(bf16), CORE_BIT).astype(f32)
            return kept[0] + cross(kept[1].astype(bf16), PAIR_BIT).astype(f32)

        small = jnp.concatenate(
            [
                ln_gain.reshape(-1),
                ln_bias.reshape(-1),
                b_fo.reshape(-1),
                b_in.reshape(-1),
                segment_ids.astype(bf16).reshape(-1),
            ]
        )[None]
        for b in [CORE_BIT, PAIR_BIT] + deep_order:
            arrived = cross(small, b)
            flag = bit(b)
            small = jnp.concatenate(
                [jnp.where(flag, arrived, small), jnp.where(flag, small, arrived)]
            )
        small_bits = ([CORE_BIT, PAIR_BIT] + deep_order)[::-1]
        small = arrange(small.reshape([2] * bits + [-1]), small_bits, every).reshape(count, -1)
        span = LAYERS * rows

        def vector(offset, depth):
            first = offset * span + depth * rows
            return small[:, first : first + rows].reshape(-1).astype(f32)

        gains = [vector(0, depth) for depth in range(LAYERS)]
        shifts = [vector(1, depth) for depth in range(LAYERS)]
        out_shifts = [vector(2, depth) for depth in range(LAYERS)]

        def own_units(value):
            by_bit = value.reshape([2] * bits + [-1])
            have = list(every)
            for b in (PAIR_BIT, CORE_BIT):
                by_bit = half(by_bit, have.index(b), True, b)
                have.remove(b)
            return arrange(by_bit, have, unit_bits).reshape(-1)

        unit_shifts = [
            own_units(small[:, 3 * span + depth * units : 3 * span + (depth + 1) * units]).astype(
                f32
            )
            for depth in range(LAYERS)
        ]
        all_ids = small[:, 3 * span + LAYERS * units :].astype(jnp.int32)
        relative = [0, 1 << PAIR_BIT, 1 << CORE_BIT, (1 << PAIR_BIT) | (1 << CORE_BIT)]
        ids = jnp.concatenate(
            [lax.dynamic_slice_in_dim(all_ids, device ^ r, 1, 0) for r in relative]
        )
        cosine, sine_table = rotary_tables(positions_of(ids), ROT)
        allowed = attention_mask(ids)[:, None]

        def reach(columns):
            value = columns
            mine, away = half(value, 0, True, CORE_BIT), half(value, 0, False, CORE_BIT)
            value = pair_up(mine, cross(away, CORE_BIT), CORE_BIT)
            mine, away = half(value, 1, True, PAIR_BIT), half(value, 1, False, PAIR_BIT)
            value = pair_up(mine, cross(away, PAIR_BIT), PAIR_BIT)
            return value

        def deep(columns):
            value = gather(reach(columns), deep_order)
            have = deep_order[::-1] + [PAIR_BIT, CORE_BIT]
            return arrange(value, have, every).reshape(width, -1)

        def qkv_columns(value):
            parts = value.reshape(rows, 3, 2, 2, 2, 2 * HEAD)
            return parts.transpose(2, 4, 0, 1, 3, 5).reshape(2, 2, rows, 3 * share_width)

        def unit_columns(value):
            parts = value.reshape([rows] + [2] * bits + [units])
            where = {b: 1 + i for i, b in enumerate(every)}
            order = [where[CORE_BIT], where[PAIR_BIT], 0] + [where[b] for b in unit_bits]
            return parts.transpose(order + [bits + 1]).reshape(2, 2, rows, share_units)

        def fetch(depth):
            attn_in = deep(qkv_columns(w_qkv[depth]))
            mlp_in = deep(unit_columns(w_in[depth]))
            rows_out = lax.ppermute(w_out[depth], AXES, exchange)
            wide = gather(jnp.concatenate([w_fo[depth], rows_out]), wide_order)
            have = wide_order[::-1]
            mlp_back = arrange(wide[..., :units, :], have, unit_bits).reshape(share_units, width)
            attn_back = arrange(wide[..., units:, :], have, head_order).reshape(
                share_width, width
            )
            return attn_in, attn_back, mlp_in, mlp_back

        heads_shape = (4, seq_len, HEADS // 4, HEAD)
        scale = HEAD ** (-0.5)

        def scores_of(rot_query, rot_key):
            scores = (
                jnp.einsum("gshe,gthe->ghst", rot_query, rot_key, preferred_element_type=f32)
                * scale
            )
            return jnp.where(allowed, scores, masked_fill)

        def forward(hidden, weights, depth):
            attn_in, attn_back, mlp_in, mlp_back = weights
            centered, _ = norm_stats(hidden)
            normed = spread((centered * gains[depth] + shifts[depth]).astype(bf16))
            projected = jnp.dot(normed, attn_in, preferred_element_type=f32)
            query = projected[:, :share_width].reshape(heads_shape)
            key = projected[:, share_width : 2 * share_width].reshape(heads_shape)
            value_low = projected[:, 2 * share_width :].reshape(heads_shape).astype(bf16)
            rot_query = rotate(query, cosine, sine_table, ROT).astype(bf16)
            rot_key = rotate(key, cosine, sine_table, ROT).astype(bf16)
            scores = scores_of(rot_query, rot_key)
            row_max = jnp.max(scores, axis=-1, keepdims=True)
            exponent = jnp.exp(scores - row_max)
            row_total = jnp.sum(exponent, axis=-1, keepdims=True)
            probs = (exponent / row_total).astype(bf16)
            attended = jnp.einsum("ghst,gthe->gshe", probs, value_low, preferred_element_type=f32)
            attended = attended.reshape(4 * seq_len, share_width).astype(bf16)
            pre = jnp.dot(normed, mlp_in, preferred_element_type=f32) + unit_shifts[depth]
            act = gelu_tanh(pre).astype(bf16)
            partial = jnp.dot(attended, attn_back, preferred_element_type=f32) + jnp.dot(
                act, mlp_back, preferred_element_type=f32
            )
            kept = (
                hidden,
                normed,
                rot_query,
                rot_key,
                value_low,
                row_max,
                row_total,
                attended,
                pre,
                act,
            )
            return kept, hidden + collect(partial) + out_shifts[depth]

        def deliver_deep(left, right, restore):
            top, order = deep_order[-1], deep_order[::-1]
            size = width // 2
            begin = jnp.where(bit(top), size, 0)
            away = lax.dynamic_slice_in_dim(left, size - begin, size, 1)
            mine = lax.dynamic_slice_in_dim(left, begin, size, 1)
            sent = cross(jnp.dot(away.T, right, preferred_element_type=f32).astype(bf16), top)
            value = jnp.dot(mine.T, right, preferred_element_type=f32) + sent.astype(f32)
            have = [b for b in every if b != top]
            value = value.reshape([2] * len(have) + [rows, -1])
            for b in order[1:]:
                value = fold(value, have.index(b), b)
                have.remove(b)
            value = value.astype(bf16)
            arrived = cross(half(value, 0, False, PAIR_BIT), PAIR_BIT)
            value = pair_up(half(value, 0, True, PAIR_BIT), arrived, PAIR_BIT)
            arrived = cross(half(value, 1, False, CORE_BIT), CORE_BIT)
            value = pair_up(half(value, 1, True, CORE_BIT), arrived, CORE_BIT)
            return restore(value.astype(f32))

        def restore_qkv(value):
            parts = value.reshape(2, 2, rows, 3, 2, 2 * HEAD)
            return parts.transpose(2, 3, 0, 4, 1, 5).reshape(rows, 3 * width)

        def restore_units(value):
            parts = value.reshape([2, 2, rows] + [2] * len(unit_bits) + [units])
            where = {b: 3 + i for i, b in enumerate(unit_bits)}
            where[CORE_BIT], where[PAIR_BIT] = 0, 1
            order = [2] + [where[b] for b in every] + [parts.ndim - 1]
            return parts.transpose(order).reshape(rows, units * count)

        def deliver_wide(act, attended, grad_low):
            top, order = wide_order[-1], wide_order[::-1]
            size = share_units // 2
            begin = jnp.where(bit(top), size, 0)
            away = lax.dynamic_slice_in_dim(act, size - begin, size, 1)
            mine = lax.dynamic_slice_in_dim(act, begin, size, 1)
            have = unit_bits[1:]
            heads_part = jnp.dot(attended.T, grad_low, preferred_element_type=f32)
            heads_part = arrange(
                heads_part.reshape([2] * len(head_order) + [rows, width]), head_order, unit_bits
            )

            def whole(units_part, heads_half):
                units_part = units_part.reshape([2] * len(have) + [units, width])
                return jnp.concatenate([units_part, heads_half], axis=len(have))

            sent = whole(
                jnp.dot(away.T, grad_low, preferred_element_type=f32).astype(bf16),
                half(heads_part, 0, False, top).astype(bf16),
            )
            arrived = cross(sent, top)
            value = whole(
                jnp.dot(mine.T, grad_low, preferred_element_type=f32),
                half(heads_part, 0, True, top),
            ) + arrived.astype(f32)
            have = list(have)
            for b in order[1:]:
                value = fold(value, have.index(b), b)
                have.remove(b)
            rows_out = lax.ppermute(value[units:].astype(bf16), AXES, exchange).astype(f32)
            return value[:units], rows_out

        def backward(grad, weights, kept, depth):
            attn_in, attn_back, mlp_in, mlp_back = weights
            (
                hidden,
                normed,
                rot_query,
                rot_key,
                value_low,
                row_max,
                row_total,
                attended,
                pre,
                act,
            ) = kept
            own_low = grad.astype(bf16)
            d_shift_out = jnp.sum(own_low, axis=0, dtype=f32)
            grad_low = spread(own_low)
            d_fo, d_out = deliver_wide(act, attended, grad_low)
            d_act = jnp.dot(grad_low, mlp_back.T, preferred_element_type=f32)
            d_pre_wide = d_act * gelu_slope(pre)
            d_pre = d_pre_wide.astype(bf16)
            d_unit_shift = jnp.sum(d_pre, axis=0, dtype=f32)
            d_in = deliver_deep(normed, d_pre, restore_units)
            d_attended = (
                jnp.dot(grad_low, attn_back.T, preferred_element_type=f32)
                .astype(bf16)
                .reshape(heads_shape)
            )
            probs_full = jnp.exp(scores_of(rot_query, rot_key) - row_max) / row_total
            d_values = jnp.einsum(
                "ghst,gshe->gthe", probs_full.astype(bf16), d_attended, preferred_element_type=f32
            )
            d_probs = jnp.einsum(
                "gshe,gthe->ghst", d_attended, value_low, preferred_element_type=f32
            )
            row_dot = jnp.sum(probs_full * d_probs, axis=-1, keepdims=True)
            d_scores = (probs_full * (d_probs - row_dot)).astype(bf16)
            d_query = (
                jnp.einsum("ghst,gthe->gshe", d_scores, rot_key, preferred_element_type=f32) * scale
            )
            d_key = (
                jnp.einsum("ghst,gshe->gthe", d_scores, rot_query, preferred_element_type=f32)
                * scale
            )
            d_projected = jnp.concatenate(
                [
                    rotate(d_query, cosine, -sine_table, ROT).reshape(-1, share_width),
                    rotate(d_key, cosine, -sine_table, ROT).reshape(-1, share_width),
                    d_values.reshape(-1, share_width),
                ],
                axis=1,
            ).astype(bf16)
            d_qkv = deliver_deep(normed, d_projected, restore_qkv)
            partial = jnp.dot(d_projected, attn_in.T, preferred_element_type=f32) + jnp.dot(
                d_pre, mlp_in.T, preferred_element_type=f32
            )
            d_normed = collect(partial)
            centered, spread_scale = norm_stats(hidden)
            d_gain = jnp.sum(d_normed * centered, axis=0)
            d_shift = jnp.sum(d_normed, axis=0)
            d_centered = d_normed * gains[depth]
            grad = grad + spread_scale * (
                d_centered
                - jnp.mean(d_centered, axis=-1, keepdims=True)
                - centered * jnp.mean(d_centered * centered, axis=-1, keepdims=True)
            )
            return grad, (d_gain, d_shift, d_shift_out, d_unit_shift), (d_qkv, d_out, d_in, d_fo)

        hidden = tokens[0].astype(f32)
        saved, weights = [], []
        for depth in range(LAYERS):
            weights.append(fetch(depth))
            kept, hidden = forward(hidden, weights[depth], depth)
            saved.append(kept)
        layer_out = hidden.astype(bf16)[None]
        grad = cotangent[0].astype(f32)
        vectors, owned = [None] * LAYERS, [None] * LAYERS
        for depth in range(LAYERS - 1, -1, -1):
            grad, vectors[depth], owned[depth] = backward(
                grad, weights[depth], saved[depth], depth
            )

        def unit_rows(value):
            by_bit = value.reshape([2] * len(unit_bits) + [units])
            have = list(unit_bits)
            for b in (PAIR_BIT, CORE_BIT):
                zero = jnp.zeros_like(by_bit)
                flag = bit(b)
                by_bit = jnp.stack(
                    [jnp.where(flag, zero, by_bit), jnp.where(flag, by_bit, zero)]
                )
                have = [b] + have
            return arrange(by_bit, have, every).reshape(count, units)

        table = jnp.concatenate(
            [vectors[depth][kind].reshape(count, rows) for kind in range(3) for depth in range(LAYERS)]
            + [unit_rows(vectors[depth][3]) for depth in range(LAYERS)],
            axis=1,
        )
        have = list(every)
        table = table.reshape([2] * bits + [-1])
        for b in deep_order[::-1] + [PAIR_BIT, CORE_BIT]:
            axis = have.index(b)
            arrived = cross(half(table, axis, False, b), b)
            table = half(table, axis, True, b) + arrived
            have.remove(b)

        def own_vector(kind):
            return jnp.stack(
                [
                    table[(kind * LAYERS + depth) * rows : (kind * LAYERS + depth + 1) * rows]
                    for depth in range(LAYERS)
                ]
            )

        d_b_in = table[3 * span :].reshape(LAYERS, units)
        return (
            layer_out,
            grad[None],
            own_vector(0),
            own_vector(1),
            jnp.stack([owned[depth][0] for depth in range(LAYERS)]),
            jnp.stack([owned[depth][1] for depth in range(LAYERS)]),
            jnp.stack([owned[depth][2] for depth in range(LAYERS)]),
            d_b_in,
            jnp.stack([owned[depth][3] for depth in range(LAYERS)]),
            own_vector(2),
        )

    return program


def solution(mesh):
    batch = P(AXES, None, None)
    columns = P(None, AXES)
    matrix = P(None, AXES, None)
    return jax.shard_map(
        build(mesh),
        mesh=mesh,
        in_specs=(
            batch,
            P(AXES, None),
            batch,
            columns,
            columns,
            matrix,
            matrix,
            matrix,
            columns,
            matrix,
            columns,
        ),
        out_specs=(
            batch,
            batch,
            columns,
            columns,
            matrix,
            matrix,
            matrix,
            columns,
            matrix,
            columns,
        ),
        check_vma=False,
    )
```

```python
import functools

import jax
import jax.numpy as jnp
from jax import lax
from jax.experimental import pallas as pl
from jax.experimental.pallas import tpu as pltpu
from jax.sharding import PartitionSpec as P

HEADS = 16
HEAD = 64
ROT = 32
LAYERS = 2
AXES = ("dp", "fsdp")

CORE_BIT = 0
PAIR_BIT = 2
FIRST_BIT = 3

layer_eps = 1e-05
gelu_scale = 0.7978845608028654
masked_fill = -1000000000.0
f32 = jnp.float32
bf16 = jnp.bfloat16


def gelu_and_slope(values):
    inner = jnp.tanh(gelu_scale * (values + 0.044715 * values * values * values))
    slope = 0.5 * (1.0 + inner) + 0.5 * values * (1.0 - inner * inner) * gelu_scale * (
        1.0 + 3.0 * 0.044715 * values * values
    )
    return 0.5 * values * (1.0 + inner), slope


def sequence_tables(segment_ids):
    length = segment_ids.shape[-1]
    index_grid = lax.broadcasted_iota(jnp.int32, segment_ids.shape, 1)
    before = segment_ids[:, None, :] < segment_ids[:, :, None]
    begin = jnp.sum(before, axis=-1, dtype=jnp.int32)
    lane = jnp.arange(2 * HEAD) % HEAD
    half_rot = ROT // 2
    frequency = 10000.0 ** (-((lane % half_rot).astype(f32) * 2.0 / ROT))
    frequency = jnp.where(lane < ROT, frequency, 0.0)
    angles = (index_grid - begin).astype(f32)[..., None] * frequency
    start = jnp.broadcast_to(begin.astype(f32)[..., None], segment_ids.shape + (2 * HEAD,))
    return jnp.concatenate([jnp.cos(angles), jnp.sin(angles), start], axis=-1).reshape(
        -1, 6 * HEAD
    )


def norm_stats(hidden):
    mean_value = jnp.mean(hidden, axis=-1, keepdims=True)
    centered = hidden - mean_value
    variance = jnp.mean(centered * centered, axis=-1, keepdims=True)
    scale = lax.rsqrt(variance + layer_eps)
    return centered * scale, scale


def turn(values, cosine, sine, sign):
    width = values.shape[1]
    half_rot = ROT // 2
    lane = lax.broadcasted_iota(jnp.int32, values.shape, 1) % HEAD
    ahead = pltpu.roll(values, width - half_rot, 1)
    behind = pltpu.roll(values, half_rot, 1)
    partner = jnp.where(lane < half_rot, -ahead, behind)
    return values * cosine + (sign * sine) * partner


def head_tables(table_ref, width):
    table = table_ref[...]
    copies = width // (2 * HEAD)
    cosine = jnp.concatenate([table[:, : 2 * HEAD]] * copies, axis=1)
    sine = jnp.concatenate([table[:, 2 * HEAD : 4 * HEAD]] * copies, axis=1)
    return cosine, sine, table[:, 4 * HEAD : 4 * HEAD + 1]


def visible(begin, length):
    row = lax.broadcasted_iota(jnp.int32, (length, length), 0)
    col = lax.broadcasted_iota(jnp.int32, (length, length), 1)
    return jnp.logical_and(col <= row, col.astype(f32) >= begin)


def only_head(values, head):
    lane = lax.broadcasted_iota(jnp.int32, values.shape, 1) // HEAD
    return jnp.where(lane == head, values, jnp.zeros_like(values))


def dot_last(left, right):
    return lax.dot_general(left, right, (((1,), (1,)), ((), ())), preferred_element_type=f32)


def dot_first(left, right):
    return lax.dot_general(left, right, (((0,), (0,)), ((), ())), preferred_element_type=f32)


def attend_kernel(normed_ref, weight_ref, table_ref, turned_ref, stats_ref, attended_ref):
    length = normed_ref.shape[0]
    width = attended_ref.shape[1]
    cosine, sine, begin = head_tables(table_ref, width)
    projected = jnp.dot(normed_ref[...], weight_ref[...], preferred_element_type=f32)
    query = turn(projected[:, :width], cosine, sine, 1.0).astype(bf16)
    key = turn(projected[:, width : 2 * width], cosine, sine, 1.0).astype(bf16)
    value = projected[:, 2 * width :].astype(bf16)
    turned_ref[:, :width] = query
    turned_ref[:, width : 2 * width] = key
    turned_ref[:, 2 * width :] = value
    seen = visible(begin, length)
    stats_lane = lax.broadcasted_iota(jnp.int32, stats_ref.shape, 1)
    stats = jnp.zeros(stats_ref.shape, f32)
    total = jnp.zeros((length, width), f32)
    for head in range(width // HEAD):
        scores = dot_last(only_head(query, head), key) * HEAD ** (-0.5)
        scores = jnp.where(seen, scores, masked_fill)
        row_max = jnp.max(scores, axis=1, keepdims=True)
        exponent = jnp.exp(scores - row_max)
        row_total = jnp.sum(exponent, axis=1, keepdims=True)
        probs = (exponent / row_total).astype(bf16)
        total += jnp.dot(probs, only_head(value, head), preferred_element_type=f32)
        stats = jnp.where(stats_lane == head, row_max, stats)
        stats = jnp.where(stats_lane == head + HEADS, row_total, stats)
    stats_ref[...] = stats
    attended_ref[...] = total.astype(bf16)


def attend_back_kernel(grad_ref, weight_ref, table_ref, turned_ref, stats_ref, out_ref):
    length = grad_ref.shape[0]
    width = weight_ref.shape[0]
    cosine, sine, begin = head_tables(table_ref, width)
    d_attended = dot_last(grad_ref[...], weight_ref[...]).astype(bf16)
    query = turned_ref[:, :width]
    key = turned_ref[:, width : 2 * width]
    value = turned_ref[:, 2 * width :]
    seen = visible(begin, length)
    stats = stats_ref[...]
    d_query = jnp.zeros((length, width), f32)
    d_key = jnp.zeros((length, width), f32)
    d_value = jnp.zeros((length, width), f32)
    for head in range(width // HEAD):
        query_head = only_head(query, head)
        scores = dot_last(query_head, key) * HEAD ** (-0.5)
        scores = jnp.where(seen, scores, masked_fill)
        row_max = stats[:, head : head + 1]
        row_total = stats[:, head + HEADS : head + HEADS + 1]
        probs = jnp.exp(scores - row_max) / row_total
        d_head = only_head(d_attended, head)
        d_value += dot_first(probs.astype(bf16), d_head)
        d_probs = dot_last(d_head, value)
        row_dot = jnp.sum(probs * d_probs, axis=1, keepdims=True)
        d_scores = (probs * (d_probs - row_dot)).astype(bf16)
        d_query += jnp.dot(d_scores, only_head(key, head), preferred_element_type=f32)
        d_key += dot_first(d_scores, query_head)
    out_ref[:, :width] = turn(d_query * HEAD ** (-0.5), cosine, sine, -1.0).astype(bf16)
    out_ref[:, width : 2 * width] = turn(d_key * HEAD ** (-0.5), cosine, sine, -1.0).astype(bf16)
    out_ref[:, 2 * width :] = d_value.astype(bf16)


def by_sequence(kernel, length, operands, whole, results):
    count = operands[0].shape[0] // length
    specs = [
        pl.BlockSpec(value.shape, lambda i: (0, 0))
        if at in whole
        else pl.BlockSpec((length, value.shape[1]), lambda i: (i, 0))
        for at, value in enumerate(operands)
    ]
    moved = sum(value.size * value.dtype.itemsize for value in operands)
    moved += sum(value.size * value.dtype.itemsize for value in results)
    return pl.pallas_call(
        kernel,
        grid=(count,),
        in_specs=specs,
        out_specs=[pl.BlockSpec((length, value.shape[1]), lambda i: (i, 0)) for value in results],
        out_shape=results,
        compiler_params=pltpu.CompilerParams(vmem_limit_bytes=32 << 20),
        cost_estimate=pl.CostEstimate(
            flops=0, bytes_accessed=1024, transcendentals=0
        ),
    )(*operands)


def place_kernel(cuts, where_ref, *refs):
    pieces, outs = refs[: -len(cuts)], refs[-len(cuts) :]
    at = 0
    for (top, bottom), out_ref in zip(cuts, outs):
        for piece_ref in pieces:
            for block in range(piece_ref.shape[0]):
                out_ref[pl.ds(where_ref[at], 1)] = piece_ref[
                    pl.ds(block, 1), pl.ds(top, bottom - top), :
                ]
                at += 1


def place(pieces, where, cuts):
    blocks = sum(piece.shape[0] for piece in pieces)
    width = pieces[0].shape[2]
    placed = pl.pallas_call(
        functools.partial(place_kernel, cuts),
        in_specs=[pl.BlockSpec(memory_space=pltpu.SMEM)]
        + [pl.BlockSpec(memory_space=pltpu.VMEM)] * len(pieces),
        out_specs=[pl.BlockSpec(memory_space=pltpu.VMEM)] * len(cuts),
        out_shape=[
            jax.ShapeDtypeStruct((blocks, bottom - top, width), pieces[0].dtype)
            for top, bottom in cuts
        ],
        compiler_params=pltpu.CompilerParams(vmem_limit_bytes=40 << 20),
        cost_estimate=pl.CostEstimate(flops=0, bytes_accessed=1024, transcendentals=0),
    )(where, *pieces)
    return [value.reshape(-1, width) for value in placed]


def build(mesh):
    count = mesh.shape["dp"] * mesh.shape["fsdp"]
    bits = count.bit_length() - 1
    head_bits = HEADS.bit_length() - 1
    every = list(range(bits - 1, -1, -1))
    shared = [b for b in every if b not in (CORE_BIT, PAIR_BIT)]
    others = [b for b in shared if b != FIRST_BIT]
    steps = len(others)
    crossing = [
        [
            (i, i ^ (1 << (others[::-1] if (i >> CORE_BIT) & 1 else others)[step]))
            for i in range(count)
        ]
        for step in range(steps)
    ]
    unit_bits = others[::-1] + [FIRST_BIT]
    stands = list(range(bits))
    for share_bit, head_bit in ((PAIR_BIT, 1), (CORE_BIT, 3)):
        target = bits - head_bits + head_bit
        if target != share_bit:
            stands[share_bit], stands[target] = target, share_bit
    exchange = [
        (i, sum(((i >> stands[b]) & 1) << b for b in range(bits))) for i in range(count)
    ]
    head_order = [stands[b] for b in every if stands[b] not in (CORE_BIT, PAIR_BIT)]

    def program(
        tokens, segment_ids, cotangent, ln_gain, ln_bias, w_qkv, w_out, w_in, b_in, w_fo, b_fo
    ):
        device = lax.axis_index(AXES)
        seq_len, width = tokens.shape[1:]
        rows = w_qkv.shape[1]
        units = w_fo.shape[1]
        share_units = units * count // 4
        share_width = width // 4
        history = {}

        def pin(value, *earlier):
            return lax.optimization_barrier((value,) + earlier)[0]

        def flag(b):
            return (device >> b) & 1

        def send(value, way):
            pairs = way if isinstance(way, list) else [(i, i ^ (1 << way)) for i in range(count)]
            return lax.ppermute(value, AXES, pairs)

        def half(value, axis, own, b):
            return lax.dynamic_index_in_dim(
                value, flag(b) if own else 1 - flag(b), axis, keepdims=False
            )

        def pair_up(mine, other, b):
            high = flag(b) == 1
            return jnp.stack([jnp.where(high, other, mine), jnp.where(high, mine, other)])

        def arrange(value, have, want):
            rest = list(range(len(have), value.ndim))
            return value.transpose([have.index(b) for b in want] + rest)

        def position(order, mask):
            other = device ^ mask
            place_of = 0
            for b in order:
                place_of = 2 * place_of + ((other >> b) & 1)
            return place_of

        def cross(value, way):
            past = history.setdefault("first" if way == FIRST_BIT else "others", [])
            depth = 1 if way == FIRST_BIT else 2
            if len(past) >= depth:
                value = pin(value, past[-depth])
            arrived = send(value, way)
            past.append(arrived)
            return arrived

        odd = flag(CORE_BIT) == 1

        def step_mask(step):
            return jnp.where(odd, 1 << others[::-1][step], 1 << others[step])

        def masks(found, order):
            for mask in order:
                found = found + [m | mask for m in found]
            return found

        gather_masks = [1 << FIRST_BIT] + [step_mask(step) for step in range(steps)]
        share_masks = masks([0], [1 << CORE_BIT, 1 << PAIR_BIT])

        def gather(value):
            for at, way in enumerate([FIRST_BIT] + crossing):
                arrived = cross(value, way)
                if at == steps:
                    yield [value, arrived]
                else:
                    yield arrived
                    value = jnp.concatenate([value, arrived])

        def blocks_of(value, have, found):
            taken = []
            for mask in found:
                other = device ^ mask
                starts = [
                    (other >> have[axis]) & 1 if axis < len(have) and have[axis] in others else 0
                    for axis in range(value.ndim)
                ]
                sizes = [
                    1 if axis < len(have) and have[axis] in others else value.shape[axis]
                    for axis in range(value.ndim)
                ]
                block = lax.dynamic_slice(value, starts, sizes)
                taken.append(
                    block.reshape(
                        [value.shape[axis] for axis in range(value.ndim) if sizes[axis] > 1 or not (axis < len(have) and have[axis] in others)]
                    )
                )
            return jnp.stack(taken)

        def scatter(value, have):
            near = masks([0], [step_mask(step) for step in range(steps - 1)])
            far = [m | step_mask(steps - 1) for m in near]
            arrived = cross(blocks_of(value, have, far).astype(bf16), crossing[-1])
            own = blocks_of(value, have, near)
            yield arrived
            value = own.astype(f32) + arrived.astype(f32)
            for step in range(steps - 2, -1, -1):
                middle = value.shape[0] // 2
                arrived = cross(value[middle:].astype(bf16), crossing[step])
                yield arrived
                value = value[:middle] + arrived.astype(f32)
            value = value[0]
            axis = [b for b in have if b not in others].index(FIRST_BIT)
            arrived = cross(half(value, axis, False, FIRST_BIT).astype(bf16), FIRST_BIT)
            yield arrived
            return half(value, axis, True, FIRST_BIT) + arrived.astype(f32)

        def spread(value):
            pair = jnp.concatenate([value, send(value, PAIR_BIT)])
            return jnp.concatenate([pair, send(pair, CORE_BIT)])

        def collect(partial):
            parts = partial.reshape(2, 2 * seq_len, width)
            kept = parts[0] + send(parts[1].astype(bf16), CORE_BIT).astype(f32)
            kept = kept.reshape(2, seq_len, width)
            return kept[0] + send(kept[1].astype(bf16), PAIR_BIT).astype(f32)

        def qkv_columns(value):
            parts = value.reshape(rows, 3, 2, 2, 2, 2 * HEAD)
            return parts.transpose(2, 4, 0, 1, 3, 5).reshape(2, 2, rows, 3 * share_width)

        def unit_columns(value):
            parts = value.reshape([rows] + [2] * bits + [units])
            where = {b: 1 + i for i, b in enumerate(every)}
            order = [where[CORE_BIT], where[PAIR_BIT], 0] + [where[b] for b in unit_bits]
            return parts.transpose(order + [bits + 1]).reshape(2, 2, rows, share_units)

        def reach(attn_part, mlp_part):
            columns = jnp.concatenate([qkv_columns(attn_part), unit_columns(mlp_part)], axis=-1)
            mine = half(columns, 0, True, CORE_BIT)
            arrived = send(half(columns, 0, False, CORE_BIT), CORE_BIT)
            columns = jnp.stack([mine, arrived], axis=1)
            mine = half(columns, 0, True, PAIR_BIT)
            arrived = send(half(columns, 0, False, PAIR_BIT), PAIR_BIT)
            return jnp.concatenate([mine, arrived])

        every_mask = masks([0], gather_masks)
        deep_where = jnp.stack(
            [position(every, outer | inner) for outer in every_mask for inner in share_masks]
        )
        wide_where = jnp.stack(
            [position(unit_bits, m) for m in every_mask]
            + [position(head_order, m) for m in every_mask]
        )

        def like(columns, kind):
            return jax.ShapeDtypeStruct((4 * seq_len, columns), kind)

        def advance(chains, names):
            for name in names:
                chains[name + "="] = next(chains[name], chains.get(name + "="))
                chains[name + "#"] = chains.get(name + "#", 0) + 1

        def finish(chains, name):
            while chains.get(name + "#", 0) < 1 + steps:
                advance(chains, [name])
            return chains[name + "="]

        def finish_deep(chains, name):
            return place(finish(chains, name), deep_where, ((0, rows),))[0]

        def finish_wide(chains):
            return place(
                finish(chains, "wide"), wide_where, ((0, units), (units, units + rows))
            )

        def enter(hidden, depth):
            centered, _ = norm_stats(hidden)
            return spread((centered * gains[depth] + shifts[depth]).astype(bf16))

        def attend(normed, attn_in):
            return by_sequence(
                attend_kernel,
                seq_len,
                (normed, attn_in, tables),
                (1,),
                [like(3 * share_width, bf16), like(2 * HEAD, f32), like(share_width, bf16)],
            )

        def activate(normed, mlp_in, depth):
            pre = jnp.dot(normed, mlp_in, preferred_element_type=f32) + unit_shifts[depth]
            act, slope = gelu_and_slope(pre)
            return act.astype(bf16), slope.astype(bf16)

        def leave(hidden, attended, attn_back, act, mlp_back, depth):
            partial = jnp.dot(attended, attn_back, preferred_element_type=f32) + jnp.dot(
                act, mlp_back, preferred_element_type=f32
            )
            return hidden + collect(partial) + out_shifts[depth]

        def scatter_deep(left, right):
            value = dot_first(left, right).reshape([2] * bits + [rows, -1])
            value = yield from scatter(value, every)
            value = value.astype(bf16)
            arrived = send(half(value, 0, False, PAIR_BIT), PAIR_BIT)
            value = pair_up(half(value, 0, True, PAIR_BIT), arrived, PAIR_BIT)
            arrived = send(half(value, 1, False, CORE_BIT), CORE_BIT)
            yield pair_up(half(value, 1, True, CORE_BIT), arrived, CORE_BIT).astype(f32)

        def restore_qkv(value):
            parts = value.reshape(2, 2, rows, 3, 2, 2 * HEAD)
            return parts.transpose(2, 3, 0, 4, 1, 5).reshape(rows, 3 * width)

        def restore_units(value):
            parts = value.reshape([2, 2, rows] + [2] * len(unit_bits) + [units])
            where = {b: 3 + i for i, b in enumerate(unit_bits)}
            where[CORE_BIT], where[PAIR_BIT] = 0, 1
            order = [2] + [where[b] for b in every] + [parts.ndim - 1]
            return parts.transpose(order).reshape(rows, units * count)

        def scatter_wide(act, attended, grad_low):
            heads_part = dot_first(attended, grad_low)
            heads_part = arrange(
                heads_part.reshape([2] * len(head_order) + [rows, width]), head_order, unit_bits
            )
            units_part = dot_first(act, grad_low).reshape([2] * len(unit_bits) + [units, width])
            value = jnp.concatenate([units_part, heads_part], axis=len(unit_bits))
            value = yield from scatter(value, unit_bits)
            rows_out = send(value[units:].astype(bf16), exchange)
            yield value[:units], rows_out.astype(f32)

        def norm_all(hidden, depth):
            centered, _ = norm_stats(hidden)
            return (centered * gains[depth] + shifts[depth]).astype(bf16)

        def small_lanes():
            lane = lax.broadcasted_iota(jnp.int32, (rows, width), 1)
            spot = lax.broadcasted_iota(jnp.int32, (rows, width), 0)
            into_width = (lane == device * rows + spot).astype(bf16)
            lane = lax.broadcasted_iota(jnp.int32, (units, share_units), 1)
            spot = lax.broadcasted_iota(jnp.int32, (units, share_units), 0)
            into_units = (lane == position(unit_bits, 0) * units + spot).astype(bf16)
            thin = jnp.dot(
                jnp.concatenate([ln_gain, ln_bias, b_fo]),
                into_width,
                preferred_element_type=f32,
            )
            thick = jnp.dot(b_in, into_units, preferred_element_type=f32)
            return jnp.concatenate([thin.reshape(-1, 128), thick.reshape(-1, 128)]).astype(bf16)

        blocks0 = reach(w_qkv[0], w_in[0])
        first = {
            "qkv": gather(blocks0[:, :, : 3 * share_width]),
            "in": gather(blocks0[:, :, 3 * share_width :]),
        }
        advance(first, ["qkv"])
        tokens_all = spread(pin(tokens[0], blocks0))
        ids = spread(pin(segment_ids.astype(bf16), blocks0)).astype(jnp.int32)
        outs = send(w_out, exchange)
        first["wide"] = gather(jnp.concatenate([w_fo[0], outs[0]])[None])
        tables = sequence_tables(ids)
        small = pin(small_lanes(), blocks0)
        for b in [FIRST_BIT] + others:
            small = small + send(small, b)
        cut = 3 * LAYERS * width // 128
        unit_shifts = small[cut:].reshape(LAYERS, share_units).astype(f32)
        small = small[:cut]
        for b in (CORE_BIT, PAIR_BIT):
            small = small + send(small, b)
        small = small.reshape(3, LAYERS, width).astype(f32)
        gains, shifts, out_shifts = small[0], small[1], small[2]
        advance(first, ["in", "qkv", "wide"])
        blocks1 = reach(pin(w_qkv[1], first["in="]), pin(w_in[1], first["in="]))
        second = {
            "qkv": gather(blocks1[:, :, : 3 * share_width]),
            "in": gather(blocks1[:, :, 3 * share_width :]),
            "wide": gather(jnp.concatenate([w_fo[1], outs[1]])[None]),
        }
        advance(first, ["qkv", "in"])
        hidden0 = tokens[0].astype(f32)
        normed0 = norm_all(tokens_all.astype(f32), 0)
        attn_in0 = finish_deep(first, "qkv")
        turned0, stats0, attended0 = attend(pin(normed0, blocks1), attn_in0)
        advance(second, ["qkv"])
        advance(first, ["in", "wide"])
        mlp_in0 = finish_deep(first, "in")
        act0, slope0 = activate(pin(normed0, second["qkv="]), mlp_in0, 0)
        advance(second, ["in"])
        advance(first, ["wide"])
        advance(second, ["wide", "qkv"])
        mlp_back0, attn_back0 = finish_wide(first)
        hidden1 = leave(
            hidden0, pin(attended0, second["in="]), attn_back0, act0, mlp_back0, 0
        )
        grad_low1 = spread(pin(cotangent[0], second["in="]))
        advance(second, ["qkv", "in"])
        normed1 = enter(hidden1, 1)
        attn_in1 = finish_deep(second, "qkv")
        turned1, stats1, attended1 = attend(normed1, attn_in1)
        advance(second, ["in", "wide"])
        mlp_in1 = finish_deep(second, "in")
        act1, slope1 = activate(normed1, mlp_in1, 1)
        advance(second, ["wide"])
        mlp_back1, attn_back1 = finish_wide(second)

        def attend_back(grad_low, attn_back, turned, stats):
            return by_sequence(
                attend_back_kernel,
                seq_len,
                (grad_low, attn_back, tables, turned, stats),
                (1,),
                [like(3 * share_width, bf16)],
            )[0]

        def slope_back(grad_low, mlp_back, slope):
            d_pre = dot_last(grad_low, mlp_back) * slope.astype(f32)
            d_pre = d_pre.astype(bf16)
            return d_pre, jnp.sum(d_pre, axis=0, dtype=f32)

        def norm_back(hidden, grad, partial, depth):
            d_normed = collect(partial)
            centered, scale = norm_stats(hidden)
            d_gain = jnp.sum(d_normed * centered, axis=0)
            d_shift = jnp.sum(d_normed, axis=0)
            d_centered = d_normed * gains[depth]
            grad = grad + scale * (
                d_centered
                - jnp.mean(d_centered, axis=-1, keepdims=True)
                - centered * jnp.mean(d_centered * centered, axis=-1, keepdims=True)
            )
            return grad, d_gain, d_shift

        def column_sum(value):
            return jnp.sum(value, axis=0, dtype=f32)

        grad1 = cotangent[0].astype(f32)
        d_shift_out1 = column_sum(cotangent[0])
        back1 = {"wide": scatter_wide(act1, attended1, grad_low1)}
        advance(back1, ["wide"])
        d_pre1, d_units1 = slope_back(grad_low1, mlp_back1, slope1)
        back1["in"] = scatter_deep(normed1, d_pre1)
        advance(back1, ["in"])
        d_projected1 = attend_back(grad_low1, attn_back1, turned1, stats1)
        partial1 = dot_last(d_projected1, attn_in1) + dot_last(d_pre1, mlp_in1)
        grad0, d_gain1, d_shift1 = norm_back(hidden1, grad1, partial1, 1)
        back1["qkv"] = scatter_deep(normed1, d_projected1)
        advance(back1, ["wide", "qkv", "in", "wide", "qkv"])
        layer_out = leave(hidden1, attended1, attn_back1, act1, mlp_back1, 1).astype(bf16)
        own_low0 = grad0.astype(bf16)
        d_shift_out0 = column_sum(own_low0)
        grad_low0 = spread(own_low0)
        back0 = {"wide": scatter_wide(act0, attended0, grad_low0)}
        advance(back0, ["wide"])
        advance(back1, ["in", "qkv"])
        d_projected0 = attend_back(grad_low0, attn_back0, turned0, stats0)
        back0["qkv"] = scatter_deep(normed0, d_projected0)
        advance(back0, ["qkv"])
        d_pre0, d_units0 = slope_back(grad_low0, mlp_back0, slope0)
        back0["in"] = scatter_deep(normed0, d_pre0)
        advance(back0, ["in"])
        partial0 = dot_last(d_projected0, attn_in0) + dot_last(d_pre0, mlp_in0)
        d_tokens, d_gain0, d_shift0 = norm_back(hidden0, grad0, partial0, 0)
        for _ in range(bits):
            advance(back0, ["wide", "qkv", "in"])
            advance(back1, ["wide", "qkv", "in"])

        thin = jnp.stack([d_gain0, d_gain1, d_shift0, d_shift1, d_shift_out0, d_shift_out1])
        sums = jnp.concatenate(
            [thin.reshape(-1, 128), jnp.stack([d_units0, d_units1]).reshape(-1, 128)]
        )
        for b in [FIRST_BIT] + others:
            sums = sums + send(sums, b)
        d_units = sums[cut:].reshape(LAYERS, share_units)
        sums = sums[:cut]
        for b in (CORE_BIT, PAIR_BIT):
            sums = sums + send(sums, b)
        sums = sums.reshape(3 * LAYERS, width)
        sums = lax.dynamic_slice_in_dim(sums, device * rows, rows, 1)
        d_b_in = lax.dynamic_slice_in_dim(d_units, position(unit_bits, 0) * units, units, 1)
        return (
            layer_out[None],
            d_tokens[None],
            sums[:LAYERS],
            sums[LAYERS : 2 * LAYERS],
            jnp.stack([restore_qkv(back0["qkv="]), restore_qkv(back1["qkv="])]),
            jnp.stack([back0["wide="][1], back1["wide="][1]]),
            jnp.stack([restore_units(back0["in="]), restore_units(back1["in="])]),
            d_b_in,
            jnp.stack([back0["wide="][0], back1["wide="][0]]),
            sums[2 * LAYERS :],
        )

    return program


def solution(mesh):
    batch = P(AXES, None, None)
    columns = P(None, AXES)
    matrix = P(None, AXES, None)
    return jax.shard_map(
        build(mesh),
        mesh=mesh,
        in_specs=(
            batch,
            P(AXES, None),
            batch,
            columns,
            columns,
            matrix,
            matrix,
            matrix,
            columns,
            matrix,
            columns,
        ),
        out_specs=(
            batch,
            batch,
            columns,
            columns,
            matrix,
            matrix,
            matrix,
            columns,
            matrix,
            columns,
        ),
        check_vma=False,
    )
```

```python
import functools

import jax
import jax.numpy as jnp
from jax import lax
from jax.experimental import pallas as pl
from jax.experimental.pallas import tpu as pltpu
from jax.sharding import PartitionSpec as P

HEADS = 16
HEAD = 64
ROT = 32
LAYERS = 2
AXES = ("dp", "fsdp")

CORE_BIT = 0
PAIR_BIT = 2
FIRST_BIT = 3

layer_eps = 1e-05
gelu_scale = 0.7978845608028654
masked_fill = -1000000000.0
f32 = jnp.float32
bf16 = jnp.bfloat16


def gelu_and_slope(values):
    inner = jnp.tanh(gelu_scale * (values + 0.044715 * values * values * values))
    slope = 0.5 * (1.0 + inner) + 0.5 * values * (1.0 - inner * inner) * gelu_scale * (
        1.0 + 3.0 * 0.044715 * values * values
    )
    return 0.5 * values * (1.0 + inner), slope


def sequence_tables(segment_ids):
    length = segment_ids.shape[-1]
    index_grid = lax.broadcasted_iota(jnp.int32, segment_ids.shape, 1)
    before = segment_ids[:, None, :] < segment_ids[:, :, None]
    begin = jnp.sum(before, axis=-1, dtype=jnp.int32)
    lane = jnp.arange(2 * HEAD) % HEAD
    half_rot = ROT // 2
    frequency = 10000.0 ** (-((lane % half_rot).astype(f32) * 2.0 / ROT))
    frequency = jnp.where(lane < ROT, frequency, 0.0)
    angles = (index_grid - begin).astype(f32)[..., None] * frequency
    start = jnp.broadcast_to(begin.astype(f32)[..., None], segment_ids.shape + (2 * HEAD,))
    return jnp.concatenate([jnp.cos(angles), jnp.sin(angles), start], axis=-1).reshape(
        -1, 6 * HEAD
    )


def norm_stats(hidden):
    mean_value = jnp.mean(hidden, axis=-1, keepdims=True)
    centered = hidden - mean_value
    variance = jnp.mean(centered * centered, axis=-1, keepdims=True)
    scale = lax.rsqrt(variance + layer_eps)
    return centered * scale, scale


def turn(values, cosine, sine, sign):
    width = values.shape[1]
    half_rot = ROT // 2
    lane = lax.broadcasted_iota(jnp.int32, values.shape, 1) % HEAD
    ahead = pltpu.roll(values, width - half_rot, 1)
    behind = pltpu.roll(values, half_rot, 1)
    partner = jnp.where(lane < half_rot, -ahead, behind)
    return values * cosine + (sign * sine) * partner


def head_tables(table_ref, width):
    table = table_ref[...]
    copies = width // (2 * HEAD)
    cosine = jnp.concatenate([table[:, : 2 * HEAD]] * copies, axis=1)
    sine = jnp.concatenate([table[:, 2 * HEAD : 4 * HEAD]] * copies, axis=1)
    return cosine, sine, table[:, 4 * HEAD : 4 * HEAD + 1]


def visible(begin, length):
    row = lax.broadcasted_iota(jnp.int32, (length, length), 0)
    col = lax.broadcasted_iota(jnp.int32, (length, length), 1)
    return jnp.logical_and(col <= row, col.astype(f32) >= begin)


def only_head(values, head):
    lane = lax.broadcasted_iota(jnp.int32, values.shape, 1) // HEAD
    return jnp.where(lane == head, values, jnp.zeros_like(values))


def dot_last(left, right):
    return lax.dot_general(left, right, (((1,), (1,)), ((), ())), preferred_element_type=f32)


def dot_first(left, right):
    return lax.dot_general(left, right, (((0,), (0,)), ((), ())), preferred_element_type=f32)


def attend_kernel(normed_ref, weight_ref, table_ref, turned_ref, stats_ref, attended_ref):
    length = normed_ref.shape[0]
    width = attended_ref.shape[1]
    cosine, sine, begin = head_tables(table_ref, width)
    projected = jnp.dot(normed_ref[...], weight_ref[...], preferred_element_type=f32)
    query = turn(projected[:, :width], cosine, sine, 1.0).astype(bf16)
    key = turn(projected[:, width : 2 * width], cosine, sine, 1.0).astype(bf16)
    value = projected[:, 2 * width :].astype(bf16)
    turned_ref[:, :width] = query
    turned_ref[:, width : 2 * width] = key
    turned_ref[:, 2 * width :] = value
    seen = visible(begin, length)
    stats_lane = lax.broadcasted_iota(jnp.int32, stats_ref.shape, 1)
    stats = jnp.zeros(stats_ref.shape, f32)
    total = jnp.zeros((length, width), f32)
    for head in range(width // HEAD):
        scores = dot_last(only_head(query, head), key) * HEAD ** (-0.5)
        scores = jnp.where(seen, scores, masked_fill)
        row_max = jnp.max(scores, axis=1, keepdims=True)
        exponent = jnp.exp(scores - row_max)
        row_total = jnp.sum(exponent, axis=1, keepdims=True)
        probs = (exponent / row_total).astype(bf16)
        total += jnp.dot(probs, only_head(value, head), preferred_element_type=f32)
        stats = jnp.where(stats_lane == head, row_max, stats)
        stats = jnp.where(stats_lane == head + HEADS, row_total, stats)
    stats_ref[...] = stats
    attended_ref[...] = total.astype(bf16)


def activate_kernel(normed_ref, weight_ref, shift_ref, act_ref, slope_ref):
    pre = jnp.dot(normed_ref[...], weight_ref[...], preferred_element_type=f32) + shift_ref[...]
    act, slope = gelu_and_slope(pre)
    act_ref[...] = act.astype(bf16)
    slope_ref[...] = slope.astype(bf16)


def part_ways(value, kept_ref, away_ref):
    here = pl.program_id(0) < pl.num_programs(0) // 2

    @pl.when(here)
    def _():
        kept_ref[...] = value

    @pl.when(jnp.logical_not(here))
    def _():
        away_ref[...] = value.astype(bf16)


def leave_kernel(attended_ref, attn_back_ref, act_ref, mlp_back_ref, kept_ref, away_ref):
    value = jnp.dot(
        attended_ref[...], attn_back_ref[...], preferred_element_type=f32
    ) + jnp.dot(act_ref[...], mlp_back_ref[...], preferred_element_type=f32)
    part_ways(value, kept_ref, away_ref)


def deep_product_kernel(source_ref, left_ref, right_ref, own_ref, away_ref, whole_ref):
    whole_ref[...] = dot_first(left_ref[...], right_ref[...]).astype(bf16)
    chunks, rows, _ = own_ref.shape
    for at in range(chunks):
        for first, out_ref in ((0, own_ref), (chunks, away_ref)):
            begin = pl.multiple_of(source_ref[first + at] * rows, rows)
            out_ref[at] = whole_ref[pl.ds(begin, rows), :]


def wide_product_kernel(
    source_ref, act_ref, attended_ref, right_ref, own_ref, away_ref, units_ref, heads_ref
):
    units_ref[...] = dot_first(act_ref[...], right_ref[...]).astype(bf16)
    heads_ref[...] = dot_first(attended_ref[...], right_ref[...]).astype(bf16)
    blocks = own_ref.shape[0]
    units = units_ref.shape[0] // (2 * blocks)
    rows = heads_ref.shape[0] // (2 * blocks)
    for at in range(blocks):
        for first, out_ref in ((0, own_ref), (blocks, away_ref)):
            begin = pl.multiple_of(source_ref[first + at] * units, units)
            out_ref[at, :units] = units_ref[pl.ds(begin, units), :]
            begin = pl.multiple_of(source_ref[2 * blocks + first + at] * rows, rows)
            out_ref[at, units:] = heads_ref[pl.ds(begin, rows), :]


def product(kernel, source, lefts, right, shape, scratch):
    blocks, rows, width = shape
    tile = 256
    out = jax.ShapeDtypeStruct(shape, bf16)
    return pl.pallas_call(
        kernel,
        grid=(width // tile,),
        in_specs=[pl.BlockSpec(memory_space=pltpu.SMEM)]
        + [
            pl.BlockSpec(left.shape, lambda i: (0, 0), pipeline_mode=pl.Buffered(1))
            for left in lefts
        ]
        + [pl.BlockSpec((right.shape[0], tile), lambda i: (0, i))],
        out_specs=[pl.BlockSpec((blocks, rows, tile), lambda i: (0, 0, i))] * 2,
        out_shape=[out, out],
        scratch_shapes=[pltpu.VMEM((size, tile), bf16) for size in scratch],
        compiler_params=pltpu.CompilerParams(vmem_limit_bytes=40 << 20),
        cost_estimate=pl.CostEstimate(flops=0, bytes_accessed=1024, transcendentals=0),
    )(source, *lefts, right)


def back_kernel(
    grad_ref,
    attn_back_ref,
    mlp_back_ref,
    slope_ref,
    table_ref,
    turned_ref,
    stats_ref,
    attn_in_ref,
    mlp_in_ref,
    pre_ref,
    projected_ref,
    kept_ref,
    away_ref,
):
    length = grad_ref.shape[0]
    width = attn_back_ref.shape[0]
    cosine, sine, begin = head_tables(table_ref, width)
    d_act = dot_last(grad_ref[...], mlp_back_ref[...])
    d_pre = (d_act * slope_ref[...].astype(f32)).astype(bf16)
    pre_ref[...] = d_pre
    d_attended = dot_last(grad_ref[...], attn_back_ref[...]).astype(bf16)
    query = turned_ref[:, :width]
    key = turned_ref[:, width : 2 * width]
    value = turned_ref[:, 2 * width :]
    seen = visible(begin, length)
    stats = stats_ref[...]
    d_query = jnp.zeros((length, width), f32)
    d_key = jnp.zeros((length, width), f32)
    d_value = jnp.zeros((length, width), f32)
    for head in range(width // HEAD):
        query_head = only_head(query, head)
        scores = dot_last(query_head, key) * HEAD ** (-0.5)
        scores = jnp.where(seen, scores, masked_fill)
        row_max = stats[:, head : head + 1]
        row_total = stats[:, head + HEADS : head + HEADS + 1]
        probs = jnp.exp(scores - row_max) / row_total
        d_head = only_head(d_attended, head)
        d_value += dot_first(probs.astype(bf16), d_head)
        d_probs = dot_last(d_head, value)
        row_dot = jnp.sum(probs * d_probs, axis=1, keepdims=True)
        d_scores = (probs * (d_probs - row_dot)).astype(bf16)
        d_query += jnp.dot(d_scores, only_head(key, head), preferred_element_type=f32)
        d_key += dot_first(d_scores, query_head)
    projected_ref[:, :width] = turn(d_query * HEAD ** (-0.5), cosine, sine, -1.0).astype(bf16)
    projected_ref[:, width : 2 * width] = turn(
        d_key * HEAD ** (-0.5), cosine, sine, -1.0
    ).astype(bf16)
    projected_ref[:, 2 * width :] = d_value.astype(bf16)
    value = dot_last(projected_ref[...], attn_in_ref[...]) + dot_last(d_pre, mlp_in_ref[...])
    part_ways(value, kept_ref, away_ref)


def by_sequence(kernel, length, operands, whole, results):
    count = operands[0].shape[0] // length

    def spec(value):
        if value.shape[0] == count * length:
            return pl.BlockSpec((length, value.shape[1]), lambda i: (i, 0))
        if value.dtype == f32:
            return pl.BlockSpec((length, value.shape[1]), lambda i: (jnp.minimum(i, 1), 0))
        return pl.BlockSpec((length, value.shape[1]), lambda i: (jnp.maximum(i - 2, 0), 0))

    return pl.pallas_call(
        kernel,
        grid=(count,),
        in_specs=[
            pl.BlockSpec(value.shape, lambda i: (0, 0), pipeline_mode=pl.Buffered(1))
            if at in whole
            else pl.BlockSpec((length, value.shape[1]), lambda i: (i, 0))
            for at, value in enumerate(operands)
        ],
        out_specs=[spec(value) for value in results],
        out_shape=results,
        compiler_params=pltpu.CompilerParams(vmem_limit_bytes=48 << 20),
        cost_estimate=pl.CostEstimate(flops=0, bytes_accessed=1024, transcendentals=0),
    )(*operands)


def place_kernel(cuts, same, where_ref, *refs):
    pieces, outs = refs[: -len(cuts)], refs[-len(cuts) :]
    at = 0
    for (top, bottom, left, right), out_ref in zip(cuts, outs):
        at = 0 if same else at
        for piece_ref in pieces:
            for block in range(piece_ref.shape[0]):
                out_ref[pl.ds(where_ref[at], 1)] = piece_ref[
                    pl.ds(block, 1), pl.ds(top, bottom - top), pl.ds(left, right - left)
                ]
                at += 1


def place(pieces, where, cuts, same=False):
    blocks = sum(piece.shape[0] for piece in pieces)
    placed = pl.pallas_call(
        functools.partial(place_kernel, cuts, same),
        in_specs=[pl.BlockSpec(memory_space=pltpu.SMEM)]
        + [pl.BlockSpec(memory_space=pltpu.VMEM)] * len(pieces),
        out_specs=[pl.BlockSpec(memory_space=pltpu.VMEM)] * len(cuts),
        out_shape=[
            jax.ShapeDtypeStruct((blocks, bottom - top, right - left), pieces[0].dtype)
            for top, bottom, left, right in cuts
        ],
        compiler_params=pltpu.CompilerParams(vmem_limit_bytes=40 << 20),
        cost_estimate=pl.CostEstimate(flops=0, bytes_accessed=1024, transcendentals=0),
    )(where, *pieces)
    return [value.reshape(-1, value.shape[-1]) for value in placed]


def build(mesh):
    count = mesh.shape["dp"] * mesh.shape["fsdp"]
    bits = count.bit_length() - 1
    head_bits = HEADS.bit_length() - 1
    every = list(range(bits - 1, -1, -1))
    shared = [b for b in every if b not in (CORE_BIT, PAIR_BIT)]
    others = [b for b in shared if b != FIRST_BIT]
    steps = len(others)
    crossing = [
        [
            (i, i ^ (1 << (others[::-1] if (i >> CORE_BIT) & 1 else others)[step]))
            for i in range(count)
        ]
        for step in range(steps)
    ]
    unit_bits = others[::-1] + [FIRST_BIT]
    stands = list(range(bits))
    for share_bit, head_bit in ((PAIR_BIT, 1), (CORE_BIT, 3)):
        target = bits - head_bits + head_bit
        if target != share_bit:
            stands[share_bit], stands[target] = target, share_bit
    exchange = [
        (i, sum(((i >> stands[b]) & 1) << b for b in range(bits))) for i in range(count)
    ]
    head_order = [stands[b] for b in every if stands[b] not in (CORE_BIT, PAIR_BIT)]

    def program(
        tokens, segment_ids, cotangent, ln_gain, ln_bias, w_qkv, w_out, w_in, b_in, w_fo, b_fo
    ):
        device = lax.axis_index(AXES)
        seq_len, width = tokens.shape[1:]
        rows = w_qkv.shape[1]
        units = w_fo.shape[1]
        share_units = units * count // 4
        share_width = width // 4
        history = {}
        at_once = [2, 1]
        operand = [None]

        def pin(value, *earlier):
            return lax.optimization_barrier((value,) + earlier)[0]

        def gated(gate, value):
            return value if gate is None else pin(value, *gate)

        def flag(b):
            return (device >> b) & 1

        def send(value, way):
            pairs = way if isinstance(way, list) else [(i, i ^ (1 << way)) for i in range(count)]
            return lax.ppermute(value, AXES, pairs)

        def half(value, axis, own, b):
            return lax.dynamic_index_in_dim(
                value, flag(b) if own else 1 - flag(b), axis, keepdims=False
            )

        def pair_up(mine, other, b):
            high = flag(b) == 1
            return jnp.stack([jnp.where(high, other, mine), jnp.where(high, mine, other)])

        def arrange(value, have, want):
            rest = list(range(len(have), value.ndim))
            return value.transpose([have.index(b) for b in want] + rest)

        def position(order, mask):
            other = device ^ mask
            place_of = 0
            for b in order:
                place_of = 2 * place_of + ((other >> b) & 1)
            return place_of

        def cross(value, way):
            past = history.setdefault("first" if way == FIRST_BIT else "others", [])
            depth = at_once[way == FIRST_BIT]
            if len(past) >= depth:
                value = pin(value, past[-depth])
            operand[0] = value
            arrived = send(value, way)
            past.append(arrived)
            return arrived

        odd = flag(CORE_BIT) == 1

        def step_mask(step):
            return jnp.where(odd, 1 << others[::-1][step], 1 << others[step])

        def masks(found, order):
            for mask in order:
                found = found + [m | mask for m in found]
            return found

        gather_masks = [1 << FIRST_BIT] + [step_mask(step) for step in range(steps)]
        share_masks = masks([0], [1 << CORE_BIT, 1 << PAIR_BIT])

        def gather(value):
            for at, way in enumerate([FIRST_BIT] + crossing):
                arrived = cross(value, way)
                if at == steps:
                    yield [value, arrived]
                else:
                    arrived = gated((yield arrived), arrived)
                    value = jnp.concatenate([value, arrived])

        def scatter(own, away):
            arrived = cross(away, crossing[-1])
            for way in crossing[-2::-1] + [FIRST_BIT]:
                arrived = gated((yield arrived), arrived)
                value = (own.astype(f32) + arrived.astype(f32)).astype(bf16)
                middle = value.shape[0] // 2
                own = value[:middle]
                arrived = cross(value[middle:], way)
            arrived = gated((yield arrived), arrived)
            return own[0].astype(f32) + arrived[0].astype(f32)

        def spread(value):
            pair = jnp.concatenate([value, send(value, PAIR_BIT)])
            return jnp.concatenate([pair, send(pair, CORE_BIT)])

        def collect_core(kept, away):
            kept = (kept + send(away, CORE_BIT).astype(f32)).reshape(2, seq_len, width)
            return kept[0], kept[1].astype(bf16)

        def qkv_columns(value):
            parts = value.reshape(rows, 3, 2, 2, 2, 2 * HEAD)
            return parts.transpose(2, 4, 0, 1, 3, 5).reshape(2, 2, rows, 3 * share_width)

        def unit_columns(value):
            parts = value.reshape([rows] + [2] * bits + [units])
            where = {b: 1 + i for i, b in enumerate(every)}
            order = [where[CORE_BIT], where[PAIR_BIT], 0] + [where[b] for b in unit_bits]
            return parts.transpose(order + [bits + 1]).reshape(2, 2, rows, share_units)

        def reach(attn_part, mlp_part):
            columns = jnp.concatenate([qkv_columns(attn_part), unit_columns(mlp_part)], axis=-1)
            mine = half(columns, 0, True, CORE_BIT)
            arrived = send(half(columns, 0, False, CORE_BIT), CORE_BIT)
            columns = jnp.stack([mine, arrived], axis=1)
            mine = half(columns, 0, True, PAIR_BIT)
            arrived = send(half(columns, 0, False, PAIR_BIT), PAIR_BIT)
            return jnp.concatenate([mine, arrived])

        every_mask = masks([0], gather_masks)
        deep_where = jnp.stack(
            [position(every, outer | inner) for outer in every_mask for inner in share_masks]
        )
        wide_where = jnp.stack(
            [position(unit_bits, m) for m in every_mask]
            + [position(head_order, m) for m in every_mask]
        )

        def like(columns, kind):
            return jax.ShapeDtypeStruct((4 * seq_len, columns), kind)

        def advance(chains, names, *gate):
            for name in names:
                chains[name + "#"] = chains.get(name + "#", 0) + 1
                held = gate if gate and chains[name + "#"] > 1 else None
                try:
                    chains[name + "="] = chains[name].send(held)
                    chains[name + "<"] = operand[0]
                except StopIteration:
                    pass

        def finish(chains, name):
            while chains.get(name + "#", 0) < 1 + steps:
                advance(chains, [name])
            return chains[name + "="]

        def finish_deep(chains, name):
            pieces = finish(chains, name)
            return place(pieces, deep_where, ((0, rows, 0, pieces[0].shape[-1]),))[0]

        def finish_wide(chains):
            return place(
                finish(chains, "wide"),
                wide_where,
                ((0, units, 0, width), (units, units + rows, 0, width)),
            )

        def enter(hidden, depth):
            centered, _ = norm_stats(hidden)
            return spread((centered * gains[depth] + shifts[depth]).astype(bf16))

        def attend(normed, attn_in):
            return by_sequence(
                attend_kernel,
                seq_len,
                (normed, attn_in, tables),
                (1,),
                [like(3 * share_width, bf16), like(2 * HEAD, f32), like(share_width, bf16)],
            )

        def activate(normed, mlp_in, depth):
            return by_sequence(
                activate_kernel,
                seq_len,
                (normed, mlp_in, unit_shifts[depth][None]),
                (1, 2),
                [like(share_units, bf16), like(share_units, bf16)],
            )

        def ways():
            half_length = 2 * seq_len
            return [
                jax.ShapeDtypeStruct((half_length, width), f32),
                jax.ShapeDtypeStruct((half_length, width), bf16),
            ]

        def leave(attended, attn_back, act, mlp_back):
            return by_sequence(
                leave_kernel, seq_len, (attended, attn_back, act, mlp_back), (1, 3), ways()
            )

        def deep_product(left, right):
            keep = sum(1 << b for b in shared)
            source = jnp.stack(
                [
                    ((device ^ mask) & keep) | (pair << PAIR_BIT) | (core << CORE_BIT)
                    for mask in every_mask
                    for pair in range(2)
                    for core in range(2)
                ]
            )
            shape = (count // 2, rows, right.shape[1])
            if rows % 16:
                chunks = dot_first(left, right).astype(bf16).reshape(count, rows, -1)[source]
                own, away = chunks[: count // 2], chunks[count // 2 :]
            else:
                own, away = product(deep_product_kernel, source, (left,), right, shape, (width,))
            return [value.reshape(count // 8, 4 * rows, -1) for value in (own, away)]

        def scatter_deep(left, right):
            value = yield from scatter(*deep_product(left, right))
            value = value.astype(bf16).reshape(2, 2, rows, -1)
            arrived = send(half(value, 0, False, PAIR_BIT), PAIR_BIT)
            value = pair_up(half(value, 0, True, PAIR_BIT), arrived, PAIR_BIT)
            arrived = send(half(value, 1, False, CORE_BIT), CORE_BIT)
            yield pair_up(half(value, 1, True, CORE_BIT), arrived, CORE_BIT).astype(f32)

        def restore_qkv(value):
            parts = value.reshape(2, 2, rows, 3, 2, 2 * HEAD)
            return parts.transpose(2, 3, 0, 4, 1, 5).reshape(rows, 3 * width)

        def restore_units(value):
            parts = value.reshape([2, 2, rows] + [2] * len(unit_bits) + [units])
            where = {b: 3 + i for i, b in enumerate(unit_bits)}
            where[CORE_BIT], where[PAIR_BIT] = 0, 1
            order = [2] + [where[b] for b in every] + [parts.ndim - 1]
            return parts.transpose(order).reshape(rows, units * count)

        def wide_product(act, attended, grad_low):
            blocks = count // 4
            source = jnp.stack(
                [position(unit_bits, m) for m in every_mask]
                + [position(head_order, m) for m in every_mask]
            )
            shape = (blocks // 2, units + rows, width)
            if rows % 16:
                units_part = dot_first(act, grad_low).astype(bf16).reshape(blocks, units, width)
                heads_part = dot_first(attended, grad_low).astype(bf16).reshape(blocks, rows, width)
                value = jnp.concatenate(
                    [units_part[source[:blocks]], heads_part[source[blocks:]]], axis=1
                )
                return value[: blocks // 2], value[blocks // 2 :]
            return product(
                wide_product_kernel,
                source,
                (act, attended),
                grad_low,
                shape,
                (share_units, share_width),
            )

        def scatter_wide(act, attended, grad_low):
            value = yield from scatter(*wide_product(act, attended, grad_low))
            rows_out = send(value[units:].astype(bf16), exchange)
            yield value[:units], rows_out.astype(f32)

        def norm_all(hidden, depth):
            centered, _ = norm_stats(hidden)
            return (centered * gains[depth] + shifts[depth]).astype(bf16)

        def small_lanes():
            lane = lax.broadcasted_iota(jnp.int32, (rows, width), 1)
            spot = lax.broadcasted_iota(jnp.int32, (rows, width), 0)
            into_width = (lane == device * rows + spot).astype(bf16)
            lane = lax.broadcasted_iota(jnp.int32, (units, share_units), 1)
            spot = lax.broadcasted_iota(jnp.int32, (units, share_units), 0)
            into_units = (lane == position(unit_bits, 0) * units + spot).astype(bf16)
            thin = jnp.dot(
                jnp.concatenate([ln_gain, ln_bias, b_fo]),
                into_width,
                preferred_element_type=f32,
            )
            thick = jnp.dot(b_in, into_units, preferred_element_type=f32)
            return jnp.concatenate([thin.reshape(-1, 128), thick.reshape(-1, 128)]).astype(bf16)

        blocks0 = reach(w_qkv[0], w_in[0])
        first = {
            "qkv": gather(blocks0[:, :, : 3 * share_width]),
            "in": gather(blocks0[:, :, 3 * share_width :]),
        }
        advance(first, ["qkv"])
        qkv_arrived = first["qkv="]
        outs = send(w_out, exchange)
        first["wide"] = gather(jnp.concatenate([w_fo[0], outs[0]])[None])
        ids = spread(pin(segment_ids.astype(bf16), first["qkv<"])).astype(jnp.int32)
        tokens_all = spread(pin(tokens[0], ids))
        small = pin(small_lanes(), first["qkv<"])
        small = small + send(small, FIRST_BIT)
        advance(first, ["in", "qkv"])
        small = pin(small, first["qkv<"])
        for b in others:
            small = small + send(small, b)
        blocks1 = reach(pin(w_qkv[1], first["qkv<"]), pin(w_in[1], first["qkv<"]))
        second = {
            "deep": gather(blocks1),
            "wide": gather(jnp.concatenate([w_fo[1], outs[1]])[None]),
        }
        advance(first, ["qkv"])
        tables = sequence_tables(pin(ids, first["qkv<"]))
        cut = 3 * LAYERS * width // 128
        unit_shifts = small[cut:].reshape(LAYERS, share_units).astype(f32)
        small = pin(small[:cut], first["qkv<"])
        for b in (CORE_BIT, PAIR_BIT):
            small = small + send(small, b)
        small = small.reshape(3, LAYERS, width).astype(f32)
        gains, shifts, out_shifts = small[0], small[1], small[2]
        grad_low1 = spread(pin(cotangent[0], first["in="]))
        advance(first, ["in", "wide"])
        advance(first, ["in"])
        advance(first, ["wide"], blocks1)
        advance(second, ["deep"])
        hidden0 = tokens[0].astype(f32)
        normed0 = norm_all(
            pin(tokens_all, first["in<"], first["wide<"], second["deep<"]).astype(f32), 0
        )
        attn_in0 = finish_deep(first, "qkv")
        turned0, stats0, attended0 = attend(normed0, attn_in0)
        advance(first, ["wide"], attended0)
        advance(second, ["deep"], attended0)
        advance(second, ["wide"])
        mlp_in0 = finish_deep(first, "in")
        act0, slope0 = activate(
            pin(normed0, first["wide<"], second["deep<"], second["wide<"]), mlp_in0, 0
        )
        advance(second, ["deep"], act0)
        mlp_back0, attn_back0 = finish_wide(first)
        kept0, away0 = leave(pin(attended0, second["deep<"]), attn_back0, act0, mlp_back0)
        kept0, over0 = collect_core(kept0, away0)
        arrived0 = send(over0, PAIR_BIT)
        advance(second, ["wide"], over0)
        hidden1 = (
            hidden0 + kept0 + pin(arrived0, second["wide<"]).astype(f32) + out_shifts[0]
        )
        centered1, _ = norm_stats(hidden1)
        normed1 = (centered1 * gains[1] + shifts[1]).astype(bf16)
        other1 = send(normed1, PAIR_BIT)
        advance(second, ["wide"], normed1)
        pair1 = jnp.concatenate([normed1, pin(other1, second["wide<"])])
        normed1 = jnp.concatenate([pair1, send(pair1, CORE_BIT)])
        attn_in1, mlp_in1 = place(
            finish(second, "deep"),
            deep_where,
            ((0, rows, 0, 3 * share_width), (0, rows, 3 * share_width, 3 * share_width + share_units)),
            True,
        )
        turned1, stats1, attended1 = attend(normed1, attn_in1)
        act1, slope1 = activate(normed1, mlp_in1, 1)
        mlp_back1, attn_back1 = finish_wide(second)

        def back(grad_low, attn_back, mlp_back, slope, turned, stats, attn_in, mlp_in):
            return by_sequence(
                back_kernel,
                seq_len,
                (grad_low, attn_back, mlp_back, slope, tables, turned, stats, attn_in, mlp_in),
                (1, 2, 7, 8),
                [like(share_units, bf16), like(3 * share_width, bf16)] + ways(),
            )

        def norm_back(hidden, grad, d_normed, depth):
            centered, scale = norm_stats(hidden)
            d_gain = jnp.sum(d_normed * centered, axis=0)
            d_shift = jnp.sum(d_normed, axis=0)
            d_centered = d_normed * gains[depth]
            grad = grad + scale * (
                d_centered
                - jnp.mean(d_centered, axis=-1, keepdims=True)
                - centered * jnp.mean(d_centered * centered, axis=-1, keepdims=True)
            )
            return grad, d_gain, d_shift

        def column_sum(value):
            return jnp.sum(value, axis=0, dtype=f32)

        at_once[:] = 9, 2
        grad1 = cotangent[0].astype(f32)
        d_shift_out1 = column_sum(cotangent[0])
        back1 = {"wide": scatter_wide(act1, attended1, grad_low1)}
        advance(back1, ["wide"])
        d_pre1, d_projected1, kept1, away1 = back(
            pin(grad_low1, back1["wide<"]),
            attn_back1,
            mlp_back1,
            slope1,
            turned1,
            stats1,
            attn_in1,
            mlp_in1,
        )
        away1 = pin(away1, back1["wide="])
        kept1, over1 = collect_core(kept1, away1)
        arrived1 = send(over1, PAIR_BIT)
        advance(back1, ["wide"], away1)
        back1["in"] = scatter_deep(normed1, pin(d_pre1, over1, back1["wide<"]))
        advance(back1, ["in"])
        back1["qkv"] = scatter_deep(normed1, pin(d_projected1, back1["in<"]))
        advance(back1, ["qkv"])
        advance(back1, ["wide"], back1["in<"])
        d_normed1 = kept1 + pin(arrived1, back1["wide<"], back1["qkv<"]).astype(f32)
        grad0, d_gain1, d_shift1 = norm_back(hidden1, grad1, d_normed1, 1)
        own_low0 = grad0.astype(bf16)
        other_low0 = send(own_low0, PAIR_BIT)
        advance(back1, ["in", "qkv"], own_low0)
        pair_low0 = jnp.concatenate(
            [own_low0, pin(other_low0, back1["in="], back1["qkv<"], back1["wide<"])]
        )
        grad_low0 = jnp.concatenate([pair_low0, send(pair_low0, CORE_BIT)])
        advance(back1, ["in"], other_low0)
        back0 = {"wide": scatter_wide(act0, attended0, grad_low0)}
        advance(back0, ["wide"])
        d_pre0, d_projected0, kept0, away0 = back(
            pin(grad_low0, back0["wide<"], back1["in<"]),
            attn_back0,
            mlp_back0,
            slope0,
            turned0,
            stats0,
            attn_in0,
            mlp_in0,
        )
        away0 = pin(away0, back0["wide="], back1["in="], back1["qkv="])
        kept0, over0 = collect_core(kept0, away0)
        arrived0 = send(over0, PAIR_BIT)
        advance(back0, ["wide"], away0)
        advance(back1, ["qkv"], away0)
        back0["in"] = scatter_deep(
            normed0, pin(d_pre0, over0, back0["wide<"], back1["qkv<"])
        )
        advance(back0, ["in"])
        back0["qkv"] = scatter_deep(normed0, pin(d_projected0, back0["in<"]))
        advance(back0, ["qkv"])
        advance(back0, ["wide"], back0["in<"])
        advance(back1, ["in", "qkv"], back0["qkv<"])
        kept, away = leave(pin(attended1, back0["qkv<"]), attn_back1, act1, mlp_back1)
        kept, over = collect_core(kept, away)
        last = send(over, PAIR_BIT)
        advance(back0, ["in", "qkv"], over)
        d_normed0 = kept0 + pin(
            arrived0, back0["wide<"], back0["in<"], back0["qkv<"]
        ).astype(f32)
        d_tokens, d_gain0, d_shift0 = norm_back(hidden0, grad0, d_normed0, 0)
        advance(back0, ["in", "qkv"])
        late = back0["in<"], back0["wide<"]
        d_units1 = column_sum(pin(d_pre1, *late))
        d_units0 = column_sum(pin(d_pre0, *late))
        d_shift_out0 = column_sum(pin(own_low0, *late))
        advance(back1, ["wide"], *late)
        layer_out = hidden1 + kept + pin(last, *late).astype(f32)
        layer_out = (layer_out + out_shifts[1]).astype(bf16)
        advance(back0, ["wide"], *late)
        for _ in range(bits):
            advance(back0, ["in", "qkv", "wide"])
            advance(back1, ["wide", "in", "qkv"])

        thin = jnp.stack([d_gain0, d_gain1, d_shift0, d_shift1, d_shift_out0, d_shift_out1])
        sums = jnp.concatenate(
            [thin.reshape(-1, 128), jnp.stack([d_units0, d_units1]).reshape(-1, 128)]
        )
        sums = pin(sums, *late)
        for b in [FIRST_BIT] + others:
            sums = sums + send(sums, b)
        d_units = sums[cut:].reshape(LAYERS, share_units)
        sums = sums[:cut]
        for b in (CORE_BIT, PAIR_BIT):
            sums = sums + send(sums, b)
        sums = sums.reshape(3 * LAYERS, width)
        sums = lax.dynamic_slice_in_dim(sums, device * rows, rows, 1)
        d_b_in = lax.dynamic_slice_in_dim(d_units, position(unit_bits, 0) * units, units, 1)
        return (
            layer_out[None],
            d_tokens[None],
            sums[:LAYERS],
            sums[LAYERS : 2 * LAYERS],
            jnp.stack([restore_qkv(back0["qkv="]), restore_qkv(back1["qkv="])]),
            jnp.stack([back0["wide="][1], back1["wide="][1]]),
            jnp.stack([restore_units(back0["in="]), restore_units(back1["in="])]),
            d_b_in,
            jnp.stack([back0["wide="][0], back1["wide="][0]]),
            sums[2 * LAYERS :],
        )

    return program


def solution(mesh):
    batch = P(AXES, None, None)
    columns = P(None, AXES)
    matrix = P(None, AXES, None)
    return jax.shard_map(
        build(mesh),
        mesh=mesh,
        in_specs=(
            batch,
            P(AXES, None),
            batch,
            columns,
            columns,
            matrix,
            matrix,
            matrix,
            columns,
            matrix,
            columns,
        ),
        out_specs=(
            batch,
            batch,
            columns,
            columns,
            matrix,
            matrix,
            matrix,
            columns,
            matrix,
            columns,
        ),
        check_vma=False,
    )
```

```python
import functools

import jax
import jax.numpy as jnp
from jax import lax
from jax.experimental import pallas as pl
from jax.experimental.pallas import tpu as pltpu
from jax.sharding import PartitionSpec as P

HEADS = 16
HEAD = 64
ROT = 32
LAYERS = 2
AXES = ("dp", "fsdp")

CORE_BIT = 0
PAIR_BIT = 2
FIRST_BIT = 3

layer_eps = 1e-05
gelu_scale = 0.7978845608028654
masked_fill = -1000000000.0
f32 = jnp.float32
bf16 = jnp.bfloat16


def gelu_and_slope(values):
    inner = jnp.tanh(gelu_scale * (values + 0.044715 * values * values * values))
    slope = 0.5 * (1.0 + inner) + 0.5 * values * (1.0 - inner * inner) * gelu_scale * (
        1.0 + 3.0 * 0.044715 * values * values
    )
    return 0.5 * values * (1.0 + inner), slope


def sequence_tables(segment_ids):
    length = segment_ids.shape[-1]
    index_grid = lax.broadcasted_iota(jnp.int32, segment_ids.shape, 1)
    before = segment_ids[:, None, :] < segment_ids[:, :, None]
    begin = jnp.sum(before, axis=-1, dtype=jnp.int32)
    lane = jnp.arange(2 * HEAD) % HEAD
    half_rot = ROT // 2
    frequency = 10000.0 ** (-((lane % half_rot).astype(f32) * 2.0 / ROT))
    frequency = jnp.where(lane < ROT, frequency, 0.0)
    angles = (index_grid - begin).astype(f32)[..., None] * frequency
    start = jnp.broadcast_to(begin.astype(f32)[..., None], segment_ids.shape + (2 * HEAD,))
    return jnp.concatenate([jnp.cos(angles), jnp.sin(angles), start], axis=-1).reshape(
        -1, 6 * HEAD
    )


def norm_stats(hidden):
    mean_value = jnp.mean(hidden, axis=-1, keepdims=True)
    centered = hidden - mean_value
    variance = jnp.mean(centered * centered, axis=-1, keepdims=True)
    scale = lax.rsqrt(variance + layer_eps)
    return centered * scale, scale


def turn(values, cosine, sine, sign):
    width = values.shape[1]
    half_rot = ROT // 2
    lane = lax.broadcasted_iota(jnp.int32, values.shape, 1) % HEAD
    ahead = pltpu.roll(values, width - half_rot, 1)
    behind = pltpu.roll(values, half_rot, 1)
    partner = jnp.where(lane < half_rot, -ahead, behind)
    return values * cosine + (sign * sine) * partner


def head_tables(table_ref, width):
    table = table_ref[...]
    copies = width // (2 * HEAD)
    cosine = jnp.concatenate([table[:, : 2 * HEAD]] * copies, axis=1)
    sine = jnp.concatenate([table[:, 2 * HEAD : 4 * HEAD]] * copies, axis=1)
    return cosine, sine, table[:, 4 * HEAD : 4 * HEAD + 1]


def visible(begin, length):
    row = lax.broadcasted_iota(jnp.int32, (length, length), 0)
    col = lax.broadcasted_iota(jnp.int32, (length, length), 1)
    return jnp.logical_and(col <= row, col.astype(f32) >= begin)


def only_head(values, head):
    lane = lax.broadcasted_iota(jnp.int32, values.shape, 1) // HEAD
    return jnp.where(lane == head, values, jnp.zeros_like(values))


def dot_last(left, right):
    return lax.dot_general(left, right, (((1,), (1,)), ((), ())), preferred_element_type=f32)


def dot_first(left, right):
    return lax.dot_general(left, right, (((0,), (0,)), ((), ())), preferred_element_type=f32)


def attend_kernel(normed_ref, weight_ref, table_ref, turned_ref, stats_ref, attended_ref):
    length = normed_ref.shape[0]
    width = attended_ref.shape[1]
    cosine, sine, begin = head_tables(table_ref, width)
    projected = jnp.dot(normed_ref[...], weight_ref[...], preferred_element_type=f32)
    query = turn(projected[:, :width], cosine, sine, 1.0).astype(bf16)
    key = turn(projected[:, width : 2 * width], cosine, sine, 1.0).astype(bf16)
    value = projected[:, 2 * width :].astype(bf16)
    turned_ref[:, :width] = query
    turned_ref[:, width : 2 * width] = key
    turned_ref[:, 2 * width :] = value
    seen = visible(begin, length)
    stats_lane = lax.broadcasted_iota(jnp.int32, stats_ref.shape, 1)
    stats = jnp.zeros(stats_ref.shape, f32)
    total = jnp.zeros((length, width), f32)
    for head in range(width // HEAD):
        scores = dot_last(only_head(query, head), key) * HEAD ** (-0.5)
        scores = jnp.where(seen, scores, masked_fill)
        row_max = jnp.max(scores, axis=1, keepdims=True)
        exponent = jnp.exp(scores - row_max)
        row_total = jnp.sum(exponent, axis=1, keepdims=True)
        probs = (exponent / row_total).astype(bf16)
        total += jnp.dot(probs, only_head(value, head), preferred_element_type=f32)
        stats = jnp.where(stats_lane == head, row_max, stats)
        stats = jnp.where(stats_lane == head + HEADS, row_total, stats)
    stats_ref[...] = stats
    attended_ref[...] = total.astype(bf16)


def activate_kernel(normed_ref, weight_ref, shift_ref, act_ref, slope_ref):
    pre = jnp.dot(normed_ref[...], weight_ref[...], preferred_element_type=f32) + shift_ref[...]
    act, slope = gelu_and_slope(pre)
    act_ref[...] = act.astype(bf16)
    slope_ref[...] = slope.astype(bf16)


def part_ways(value, kept_ref, away_ref):
    here = pl.program_id(0) < pl.num_programs(0) // 2

    @pl.when(here)
    def _():
        kept_ref[...] = value

    @pl.when(jnp.logical_not(here))
    def _():
        away_ref[...] = value.astype(bf16)


def leave_kernel(attended_ref, attn_back_ref, act_ref, mlp_back_ref, kept_ref, away_ref):
    value = jnp.dot(
        attended_ref[...], attn_back_ref[...], preferred_element_type=f32
    ) + jnp.dot(act_ref[...], mlp_back_ref[...], preferred_element_type=f32)
    part_ways(value, kept_ref, away_ref)


def deep_product_kernel(source_ref, left_ref, right_ref, own_ref, away_ref, whole_ref):
    whole_ref[...] = dot_first(left_ref[...], right_ref[...]).astype(bf16)
    chunks, rows, _ = own_ref.shape
    for at in range(chunks):
        for first, out_ref in ((0, own_ref), (chunks, away_ref)):
            begin = pl.multiple_of(source_ref[first + at] * rows, rows)
            out_ref[at] = whole_ref[pl.ds(begin, rows), :]


def wide_product_kernel(
    source_ref, act_ref, attended_ref, right_ref, own_ref, away_ref, units_ref, heads_ref
):
    units_ref[...] = dot_first(act_ref[...], right_ref[...]).astype(bf16)
    heads_ref[...] = dot_first(attended_ref[...], right_ref[...]).astype(bf16)
    blocks = own_ref.shape[0]
    units = units_ref.shape[0] // (2 * blocks)
    rows = heads_ref.shape[0] // (2 * blocks)
    for at in range(blocks):
        for first, out_ref in ((0, own_ref), (blocks, away_ref)):
            begin = pl.multiple_of(source_ref[first + at] * units, units)
            out_ref[at, :units] = units_ref[pl.ds(begin, units), :]
            begin = pl.multiple_of(source_ref[2 * blocks + first + at] * rows, rows)
            out_ref[at, units:] = heads_ref[pl.ds(begin, rows), :]


def product(kernel, source, lefts, right, shape, scratch):
    blocks, rows, width = shape
    tile = 256
    out = jax.ShapeDtypeStruct(shape, bf16)
    return pl.pallas_call(
        kernel,
        grid=(width // tile,),
        in_specs=[pl.BlockSpec(memory_space=pltpu.SMEM)]
        + [
            pl.BlockSpec(left.shape, lambda i: (0, 0), pipeline_mode=pl.Buffered(1))
            for left in lefts
        ]
        + [pl.BlockSpec((right.shape[0], tile), lambda i: (0, i))],
        out_specs=[pl.BlockSpec((blocks, rows, tile), lambda i: (0, 0, i))] * 2,
        out_shape=[out, out],
        scratch_shapes=[pltpu.VMEM((size, tile), bf16) for size in scratch],
        compiler_params=pltpu.CompilerParams(vmem_limit_bytes=40 << 20),
        cost_estimate=pl.CostEstimate(flops=0, bytes_accessed=1024, transcendentals=0),
    )(source, *lefts, right)


def back_kernel(
    grad_ref,
    attn_back_ref,
    mlp_back_ref,
    slope_ref,
    table_ref,
    turned_ref,
    stats_ref,
    attn_in_ref,
    mlp_in_ref,
    pre_ref,
    projected_ref,
    kept_ref,
    away_ref,
):
    length = grad_ref.shape[0]
    width = attn_back_ref.shape[0]
    cosine, sine, begin = head_tables(table_ref, width)
    d_act = dot_last(grad_ref[...], mlp_back_ref[...])
    d_pre = (d_act * slope_ref[...].astype(f32)).astype(bf16)
    pre_ref[...] = d_pre
    d_attended = dot_last(grad_ref[...], attn_back_ref[...]).astype(bf16)
    query = turned_ref[:, :width]
    key = turned_ref[:, width : 2 * width]
    value = turned_ref[:, 2 * width :]
    seen = visible(begin, length)
    stats = stats_ref[...]
    d_query = jnp.zeros((length, width), f32)
    d_key = jnp.zeros((length, width), f32)
    d_value = jnp.zeros((length, width), f32)
    for head in range(width // HEAD):
        query_head = only_head(query, head)
        scores = dot_last(query_head, key) * HEAD ** (-0.5)
        scores = jnp.where(seen, scores, masked_fill)
        row_max = stats[:, head : head + 1]
        row_total = stats[:, head + HEADS : head + HEADS + 1]
        probs = jnp.exp(scores - row_max) / row_total
        d_head = only_head(d_attended, head)
        d_value += dot_first(probs.astype(bf16), d_head)
        d_probs = dot_last(d_head, value)
        row_dot = jnp.sum(probs * d_probs, axis=1, keepdims=True)
        d_scores = (probs * (d_probs - row_dot)).astype(bf16)
        d_query += jnp.dot(d_scores, only_head(key, head), preferred_element_type=f32)
        d_key += dot_first(d_scores, query_head)
    projected_ref[:, :width] = turn(d_query * HEAD ** (-0.5), cosine, sine, -1.0).astype(bf16)
    projected_ref[:, width : 2 * width] = turn(
        d_key * HEAD ** (-0.5), cosine, sine, -1.0
    ).astype(bf16)
    projected_ref[:, 2 * width :] = d_value.astype(bf16)
    value = dot_last(projected_ref[...], attn_in_ref[...]) + dot_last(d_pre, mlp_in_ref[...])
    part_ways(value, kept_ref, away_ref)


def by_sequence(kernel, length, operands, whole, results):
    count = operands[0].shape[0] // length

    def spec(value):
        if value.shape[0] == count * length:
            return pl.BlockSpec((length, value.shape[1]), lambda i: (i, 0))
        if value.dtype == f32:
            return pl.BlockSpec((length, value.shape[1]), lambda i: (jnp.minimum(i, 1), 0))
        return pl.BlockSpec((length, value.shape[1]), lambda i: (jnp.maximum(i - 2, 0), 0))

    return pl.pallas_call(
        kernel,
        grid=(count,),
        in_specs=[
            pl.BlockSpec(value.shape, lambda i: (0, 0), pipeline_mode=pl.Buffered(1))
            if at in whole
            else pl.BlockSpec((length, value.shape[1]), lambda i: (i, 0))
            for at, value in enumerate(operands)
        ],
        out_specs=[spec(value) for value in results],
        out_shape=results,
        compiler_params=pltpu.CompilerParams(vmem_limit_bytes=48 << 20),
        cost_estimate=pl.CostEstimate(flops=0, bytes_accessed=1024, transcendentals=0),
    )(*operands)


def place_kernel(cuts, same, where_ref, *refs):
    pieces, outs = refs[: -len(cuts)], refs[-len(cuts) :]
    at = 0
    for (top, bottom, left, right), out_ref in zip(cuts, outs):
        at = 0 if same else at
        for piece_ref in pieces:
            for block in range(piece_ref.shape[0]):
                out_ref[pl.ds(where_ref[at], 1)] = piece_ref[
                    pl.ds(block, 1), pl.ds(top, bottom - top), pl.ds(left, right - left)
                ]
                at += 1


def place(pieces, where, cuts, same=False):
    blocks = sum(piece.shape[0] for piece in pieces)
    placed = pl.pallas_call(
        functools.partial(place_kernel, cuts, same),
        in_specs=[pl.BlockSpec(memory_space=pltpu.SMEM)]
        + [pl.BlockSpec(memory_space=pltpu.VMEM)] * len(pieces),
        out_specs=[pl.BlockSpec(memory_space=pltpu.VMEM)] * len(cuts),
        out_shape=[
            jax.ShapeDtypeStruct((blocks, bottom - top, right - left), pieces[0].dtype)
            for top, bottom, left, right in cuts
        ],
        compiler_params=pltpu.CompilerParams(vmem_limit_bytes=40 << 20),
        cost_estimate=pl.CostEstimate(flops=0, bytes_accessed=1024, transcendentals=0),
    )(where, *pieces)
    return [value.reshape(-1, value.shape[-1]) for value in placed]


def build(mesh):
    count = mesh.shape["dp"] * mesh.shape["fsdp"]
    bits = count.bit_length() - 1
    head_bits = HEADS.bit_length() - 1
    every = list(range(bits - 1, -1, -1))
    shared = [b for b in every if b not in (CORE_BIT, PAIR_BIT)]
    others = [b for b in shared if b != FIRST_BIT]
    steps = len(others)
    crossing = [
        [
            (i, i ^ (1 << (others[::-1] if (i >> CORE_BIT) & 1 else others)[step]))
            for i in range(count)
        ]
        for step in range(steps)
    ]
    unit_bits = others[::-1] + [FIRST_BIT]
    stands = list(range(bits))
    for share_bit, head_bit in ((PAIR_BIT, 1), (CORE_BIT, 3)):
        target = bits - head_bits + head_bit
        if target != share_bit:
            stands[share_bit], stands[target] = target, share_bit
    exchange = [
        (i, sum(((i >> stands[b]) & 1) << b for b in range(bits))) for i in range(count)
    ]
    head_order = [stands[b] for b in every if stands[b] not in (CORE_BIT, PAIR_BIT)]

    def program(
        tokens, segment_ids, cotangent, ln_gain, ln_bias, w_qkv, w_out, w_in, b_in, w_fo, b_fo
    ):
        device = lax.axis_index(AXES)
        seq_len, width = tokens.shape[1:]
        rows = w_qkv.shape[1]
        units = w_fo.shape[1]
        share_units = units * count // 4
        share_width = width // 4
        history = {}
        at_once = [2, 1]
        operand = [None]

        def pin(value, *earlier):
            return lax.optimization_barrier((value,) + earlier)[0]

        def gated(gate, value):
            return value if gate is None else pin(value, *gate)

        def flag(b):
            return (device >> b) & 1

        def send(value, way):
            pairs = way if isinstance(way, list) else [(i, i ^ (1 << way)) for i in range(count)]
            return lax.ppermute(value, AXES, pairs)

        def half(value, axis, own, b):
            return lax.dynamic_index_in_dim(
                value, flag(b) if own else 1 - flag(b), axis, keepdims=False
            )

        def pair_up(mine, other, b):
            high = flag(b) == 1
            return jnp.stack([jnp.where(high, other, mine), jnp.where(high, mine, other)])

        def arrange(value, have, want):
            rest = list(range(len(have), value.ndim))
            return value.transpose([have.index(b) for b in want] + rest)

        def position(order, mask):
            other = device ^ mask
            place_of = 0
            for b in order:
                place_of = 2 * place_of + ((other >> b) & 1)
            return place_of

        def cross(value, way):
            past = history.setdefault("first" if way == FIRST_BIT else "others", [])
            depth = at_once[way == FIRST_BIT]
            if len(past) >= depth:
                value = pin(value, past[-depth])
            operand[0] = value
            arrived = send(value, way)
            past.append(arrived)
            return arrived

        odd = flag(CORE_BIT) == 1

        def step_mask(step):
            return jnp.where(odd, 1 << others[::-1][step], 1 << others[step])

        def masks(found, order):
            for mask in order:
                found = found + [m | mask for m in found]
            return found

        gather_masks = [1 << FIRST_BIT] + [step_mask(step) for step in range(steps)]
        share_masks = masks([0], [1 << CORE_BIT, 1 << PAIR_BIT])

        def gather(value):
            for at, way in enumerate([FIRST_BIT] + crossing):
                arrived = cross(value, way)
                if at == steps:
                    yield [value, arrived]
                else:
                    arrived = gated((yield arrived), arrived)
                    value = jnp.concatenate([value, arrived])

        def scatter(own, away):
            arrived = cross(away, crossing[-1])
            for way in crossing[-2::-1] + [FIRST_BIT]:
                arrived = gated((yield arrived), arrived)
                value = (own.astype(f32) + arrived.astype(f32)).astype(bf16)
                middle = value.shape[0] // 2
                own = value[:middle]
                arrived = cross(value[middle:], way)
            arrived = gated((yield arrived), arrived)
            return own[0].astype(f32) + arrived[0].astype(f32)

        def spread(value):
            pair = jnp.concatenate([value, send(value, PAIR_BIT)])
            return jnp.concatenate([pair, send(pair, CORE_BIT)])

        def collect_core(kept, away):
            kept = (kept + send(away, CORE_BIT).astype(f32)).reshape(2, seq_len, width)
            return kept[0], kept[1].astype(bf16)

        def qkv_columns(value):
            parts = value.reshape(rows, 3, 2, 2, 2, 2 * HEAD)
            return parts.transpose(2, 4, 0, 1, 3, 5).reshape(2, 2, rows, 3 * share_width)

        def unit_columns(value):
            parts = value.reshape([rows] + [2] * bits + [units])
            where = {b: 1 + i for i, b in enumerate(every)}
            order = [where[CORE_BIT], where[PAIR_BIT], 0] + [where[b] for b in unit_bits]
            return parts.transpose(order + [bits + 1]).reshape(2, 2, rows, share_units)

        def reach(attn_part, mlp_part):
            columns = jnp.concatenate([qkv_columns(attn_part), unit_columns(mlp_part)], axis=-1)
            mine = half(columns, 0, True, CORE_BIT)
            arrived = send(half(columns, 0, False, CORE_BIT), CORE_BIT)
            columns = jnp.stack([mine, arrived], axis=1)
            mine = half(columns, 0, True, PAIR_BIT)
            arrived = send(half(columns, 0, False, PAIR_BIT), PAIR_BIT)
            return jnp.concatenate([mine, arrived])

        every_mask = masks([0], gather_masks)
        deep_where = jnp.stack(
            [position(every, outer | inner) for outer in every_mask for inner in share_masks]
        )
        wide_where = jnp.stack(
            [position(unit_bits, m) for m in every_mask]
            + [position(head_order, m) for m in every_mask]
        )

        def like(columns, kind):
            return jax.ShapeDtypeStruct((4 * seq_len, columns), kind)

        def advance(chains, names, *gate):
            for name in names:
                chains[name + "#"] = chains.get(name + "#", 0) + 1
                held = gate if gate and chains[name + "#"] > 1 else None
                try:
                    chains[name + "="] = chains[name].send(held)
                    chains[name + "<"] = operand[0]
                except StopIteration:
                    pass

        def finish(chains, name):
            while chains.get(name + "#", 0) < 1 + steps:
                advance(chains, [name])
            return chains[name + "="]

        def finish_deep(chains, name):
            pieces = finish(chains, name)
            return place(pieces, deep_where, ((0, rows, 0, pieces[0].shape[-1]),))[0]

        def finish_wide(chains):
            return place(
                finish(chains, "wide"),
                wide_where,
                ((0, units, 0, width), (units, units + rows, 0, width)),
            )

        def enter(hidden, depth):
            centered, _ = norm_stats(hidden)
            return spread((centered * gains[depth] + shifts[depth]).astype(bf16))

        def attend(normed, attn_in):
            return by_sequence(
                attend_kernel,
                seq_len,
                (normed, attn_in, tables),
                (1,),
                [like(3 * share_width, bf16), like(2 * HEAD, f32), like(share_width, bf16)],
            )

        def activate(normed, mlp_in, depth):
            return by_sequence(
                activate_kernel,
                seq_len,
                (normed, mlp_in, unit_shifts[depth][None]),
                (1, 2),
                [like(share_units, bf16), like(share_units, bf16)],
            )

        def ways():
            half_length = 2 * seq_len
            return [
                jax.ShapeDtypeStruct((half_length, width), f32),
                jax.ShapeDtypeStruct((half_length, width), bf16),
            ]

        def leave(attended, attn_back, act, mlp_back):
            return by_sequence(
                leave_kernel, seq_len, (attended, attn_back, act, mlp_back), (1, 3), ways()
            )

        def deep_product(left, right):
            keep = sum(1 << b for b in shared)
            source = jnp.stack(
                [
                    ((device ^ mask) & keep) | (pair << PAIR_BIT) | (core << CORE_BIT)
                    for mask in every_mask
                    for pair in range(2)
                    for core in range(2)
                ]
            )
            shape = (count // 2, rows, right.shape[1])
            if rows % 16:
                chunks = dot_first(left, right).astype(bf16).reshape(count, rows, -1)[source]
                own, away = chunks[: count // 2], chunks[count // 2 :]
            else:
                own, away = product(deep_product_kernel, source, (left,), right, shape, (width,))
            return [value.reshape(count // 8, 4 * rows, -1) for value in (own, away)]

        def scatter_deep(left, right):
            value = yield from scatter(*deep_product(left, right))
            value = value.astype(bf16).reshape(2, 2, rows, -1)
            arrived = send(half(value, 0, False, PAIR_BIT), PAIR_BIT)
            value = pair_up(half(value, 0, True, PAIR_BIT), arrived, PAIR_BIT)
            arrived = send(half(value, 1, False, CORE_BIT), CORE_BIT)
            yield pair_up(half(value, 1, True, CORE_BIT), arrived, CORE_BIT).astype(f32)

        def restore_qkv(value):
            parts = value.reshape(2, 2, rows, 3, 2, 2 * HEAD)
            return parts.transpose(2, 3, 0, 4, 1, 5).reshape(rows, 3 * width)

        def restore_units(value):
            parts = value.reshape([2, 2, rows] + [2] * len(unit_bits) + [units])
            where = {b: 3 + i for i, b in enumerate(unit_bits)}
            where[CORE_BIT], where[PAIR_BIT] = 0, 1
            order = [2] + [where[b] for b in every] + [parts.ndim - 1]
            return parts.transpose(order).reshape(rows, units * count)

        def wide_product(act, attended, grad_low):
            blocks = count // 4
            source = jnp.stack(
                [position(unit_bits, m) for m in every_mask]
                + [position(head_order, m) for m in every_mask]
            )
            shape = (blocks // 2, units + rows, width)
            if rows % 16:
                units_part = dot_first(act, grad_low).astype(bf16).reshape(blocks, units, width)
                heads_part = dot_first(attended, grad_low).astype(bf16).reshape(blocks, rows, width)
                value = jnp.concatenate(
                    [units_part[source[:blocks]], heads_part[source[blocks:]]], axis=1
                )
                return value[: blocks // 2], value[blocks // 2 :]
            return product(
                wide_product_kernel,
                source,
                (act, attended),
                grad_low,
                shape,
                (share_units, share_width),
            )

        def scatter_wide(act, attended, grad_low):
            value = yield from scatter(*wide_product(act, attended, grad_low))
            rows_out = send(value[units:].astype(bf16), exchange)
            yield value[:units], rows_out.astype(f32)

        def norm_all(hidden, depth):
            centered, _ = norm_stats(hidden)
            return (centered * gains[depth] + shifts[depth]).astype(bf16)

        def small_lanes():
            lane = lax.broadcasted_iota(jnp.int32, (rows, width), 1)
            spot = lax.broadcasted_iota(jnp.int32, (rows, width), 0)
            into_width = (lane == device * rows + spot).astype(bf16)
            lane = lax.broadcasted_iota(jnp.int32, (units, share_units), 1)
            spot = lax.broadcasted_iota(jnp.int32, (units, share_units), 0)
            into_units = (lane == position(unit_bits, 0) * units + spot).astype(bf16)
            thin = jnp.dot(
                jnp.concatenate([ln_gain, ln_bias, b_fo]),
                into_width,
                preferred_element_type=f32,
            )
            thick = jnp.dot(b_in, into_units, preferred_element_type=f32)
            return jnp.concatenate([thin.reshape(-1, 128), thick.reshape(-1, 128)]).astype(bf16)

        blocks0 = reach(w_qkv[0], w_in[0])
        small = small_lanes()
        cut = 3 * LAYERS * width // 128
        thin, thick = small[:cut], small[cut:]
        for b in (CORE_BIT, PAIR_BIT):
            thin = thin + send(thin, b)
        small = jnp.concatenate([thin, thick])
        first = {
            "qkv": gather(blocks0[:, :, : 3 * share_width]),
            "in": gather(blocks0[:, :, 3 * share_width :]),
        }
        advance(first, ["qkv"])
        qkv_arrived = first["qkv="]
        outs = send(w_out, exchange)
        first["wide"] = gather(jnp.concatenate([w_fo[0], outs[0]])[None])
        ids = spread(pin(segment_ids.astype(bf16), first["qkv<"])).astype(jnp.int32)
        tokens_all = spread(pin(tokens[0], ids))
        small = pin(small, first["qkv<"])
        small = small + send(small, FIRST_BIT)
        advance(first, ["in", "qkv"])
        small = pin(small, first["qkv<"])
        for b in others:
            small = small + send(small, b)
        blocks1 = reach(pin(w_qkv[1], first["qkv<"]), pin(w_in[1], first["qkv<"]))
        second = {
            "deep": gather(blocks1),
            "wide": gather(jnp.concatenate([w_fo[1], outs[1]])[None]),
        }
        advance(first, ["qkv"])
        tables = sequence_tables(pin(ids, first["qkv<"]))
        unit_shifts = small[cut:].reshape(LAYERS, share_units).astype(f32)
        small = small[:cut]
        small = small.reshape(3, LAYERS, width).astype(f32)
        gains, shifts, out_shifts = small[0], small[1], small[2]
        grad_low1 = spread(pin(cotangent[0], first["in="]))
        advance(first, ["in", "wide"])
        advance(first, ["in"])
        advance(first, ["wide"], blocks1)
        advance(second, ["deep"])
        hidden0 = tokens[0].astype(f32)
        normed0 = norm_all(
            pin(tokens_all, first["in<"], first["wide<"], second["deep<"]).astype(f32), 0
        )
        attn_in0 = finish_deep(first, "qkv")
        turned0, stats0, attended0 = attend(normed0, attn_in0)
        advance(first, ["wide"], attended0)
        advance(second, ["deep"], attended0)
        advance(second, ["wide"])
        mlp_in0 = finish_deep(first, "in")
        act0, slope0 = activate(
            pin(normed0, first["wide<"], second["deep<"], second["wide<"]), mlp_in0, 0
        )
        advance(second, ["deep"], act0)
        mlp_back0, attn_back0 = finish_wide(first)
        kept0, away0 = leave(pin(attended0, second["deep<"]), attn_back0, act0, mlp_back0)
        kept0, over0 = collect_core(kept0, pin(away0, second["wide="]))
        arrived0 = send(over0, PAIR_BIT)
        advance(second, ["wide"], over0)
        hidden1 = (
            hidden0 + kept0 + pin(arrived0, second["wide<"]).astype(f32) + out_shifts[0]
        )
        centered1, _ = norm_stats(hidden1)
        normed1 = (centered1 * gains[1] + shifts[1]).astype(bf16)
        other1 = send(normed1, PAIR_BIT)
        advance(second, ["wide"], normed1)
        pair1 = jnp.concatenate([normed1, pin(other1, second["wide<"])])
        normed1 = jnp.concatenate([pair1, send(pair1, CORE_BIT)])
        attn_in1, mlp_in1 = place(
            finish(second, "deep"),
            deep_where,
            ((0, rows, 0, 3 * share_width), (0, rows, 3 * share_width, 3 * share_width + share_units)),
            True,
        )
        turned1, stats1, attended1 = attend(normed1, attn_in1)
        act1, slope1 = activate(normed1, mlp_in1, 1)
        mlp_back1, attn_back1 = finish_wide(second)

        def back(grad_low, attn_back, mlp_back, slope, turned, stats, attn_in, mlp_in):
            return by_sequence(
                back_kernel,
                seq_len,
                (grad_low, attn_back, mlp_back, slope, tables, turned, stats, attn_in, mlp_in),
                (1, 2, 7, 8),
                [like(share_units, bf16), like(3 * share_width, bf16)] + ways(),
            )

        def norm_back(hidden, grad, d_normed, depth):
            centered, scale = norm_stats(hidden)
            d_gain = jnp.sum(d_normed * centered, axis=0)
            d_shift = jnp.sum(d_normed, axis=0)
            d_centered = d_normed * gains[depth]
            grad = grad + scale * (
                d_centered
                - jnp.mean(d_centered, axis=-1, keepdims=True)
                - centered * jnp.mean(d_centered * centered, axis=-1, keepdims=True)
            )
            return grad, d_gain, d_shift

        def column_sum(value):
            return jnp.sum(value, axis=0, dtype=f32)

        at_once[:] = 9, 2
        grad1 = cotangent[0].astype(f32)
        d_shift_out1 = column_sum(cotangent[0])
        back1 = {"wide": scatter_wide(act1, attended1, grad_low1)}
        advance(back1, ["wide"])
        d_pre1, d_projected1, kept1, away1 = back(
            pin(grad_low1, back1["wide<"]),
            attn_back1,
            mlp_back1,
            slope1,
            turned1,
            stats1,
            attn_in1,
            mlp_in1,
        )
        away1 = pin(away1, back1["wide="])
        kept1, over1 = collect_core(kept1, away1)
        arrived1 = send(over1, PAIR_BIT)
        advance(back1, ["wide"], away1)
        back1["in"] = scatter_deep(normed1, pin(d_pre1, over1, back1["wide<"]))
        advance(back1, ["in"])
        back1["qkv"] = scatter_deep(normed1, pin(d_projected1, back1["in<"]))
        advance(back1, ["qkv"])
        advance(back1, ["wide"], back1["in<"])
        d_normed1 = kept1 + pin(arrived1, back1["wide<"], back1["qkv<"]).astype(f32)
        grad0, d_gain1, d_shift1 = norm_back(hidden1, grad1, d_normed1, 1)
        own_low0 = grad0.astype(bf16)
        other_low0 = send(own_low0, PAIR_BIT)
        advance(back1, ["in", "qkv"], own_low0)
        pair_low0 = jnp.concatenate(
            [own_low0, pin(other_low0, back1["in="], back1["qkv<"], back1["wide="])]
        )
        grad_low0 = jnp.concatenate([pair_low0, send(pair_low0, CORE_BIT)])
        advance(back1, ["in"], other_low0)
        back0 = {"wide": scatter_wide(act0, attended0, grad_low0)}
        advance(back0, ["wide"])
        d_pre0, d_projected0, kept0, away0 = back(
            pin(grad_low0, back0["wide<"], back1["in<"]),
            attn_back0,
            mlp_back0,
            slope0,
            turned0,
            stats0,
            attn_in0,
            mlp_in0,
        )
        away0 = pin(away0, back0["wide="], back1["in="], back1["qkv="])
        kept0, over0 = collect_core(kept0, away0)
        arrived0 = send(over0, PAIR_BIT)
        advance(back0, ["wide"], away0)
        advance(back1, ["qkv"], over0)
        back0["in"] = scatter_deep(
            normed0, pin(d_pre0, over0, back0["wide<"], back1["qkv<"])
        )
        advance(back0, ["in"])
        back0["qkv"] = scatter_deep(normed0, pin(d_projected0, back0["in<"]))
        advance(back0, ["qkv"])
        advance(back0, ["wide"], back0["in<"])
        advance(back1, ["in", "qkv"], back0["qkv<"])
        kept, away = leave(pin(attended1, back0["qkv<"], arrived0), attn_back1, act1, mlp_back1)
        kept, over = collect_core(kept, away)
        last = send(over, PAIR_BIT)
        advance(back0, ["in", "qkv"], over)
        d_normed0 = kept0 + pin(
            arrived0, back0["wide<"], back0["in<"], back0["qkv<"]
        ).astype(f32)
        d_tokens, d_gain0, d_shift0 = norm_back(hidden0, grad0, d_normed0, 0)
        advance(back0, ["in", "qkv"])
        late = back0["in<"], back0["wide<"]
        d_units1 = column_sum(pin(d_pre1, *late))
        d_units0 = column_sum(pin(d_pre0, *late))
        d_shift_out0 = column_sum(pin(own_low0, *late))
        advance(back1, ["wide"], *late)
        layer_out = hidden1 + kept + pin(last, *late).astype(f32)
        layer_out = (layer_out + out_shifts[1]).astype(bf16)
        advance(back0, ["wide"], *late)
        for _ in range(bits):
            advance(back0, ["in", "qkv", "wide"])
            advance(back1, ["wide", "in", "qkv"])

        thin = jnp.stack([d_gain0, d_gain1, d_shift0, d_shift1, d_shift_out0, d_shift_out1])
        sums = jnp.concatenate(
            [thin.reshape(-1, 128), jnp.stack([d_units0, d_units1]).reshape(-1, 128)]
        )
        sums = pin(sums, *late)
        for b in [FIRST_BIT] + others:
            sums = sums + send(sums, b)
        d_units = sums[cut:].reshape(LAYERS, share_units)
        sums = sums[:cut]
        for b in (CORE_BIT, PAIR_BIT):
            sums = sums + send(sums, b)
        sums = sums.reshape(3 * LAYERS, width)
        sums = lax.dynamic_slice_in_dim(sums, device * rows, rows, 1)
        d_b_in = lax.dynamic_slice_in_dim(d_units, position(unit_bits, 0) * units, units, 1)
        return (
            layer_out[None],
            d_tokens[None],
            sums[:LAYERS],
            sums[LAYERS : 2 * LAYERS],
            jnp.stack([restore_qkv(back0["qkv="]), restore_qkv(back1["qkv="])]),
            jnp.stack([back0["wide="][1], back1["wide="][1]]),
            jnp.stack([restore_units(back0["in="]), restore_units(back1["in="])]),
            d_b_in,
            jnp.stack([back0["wide="][0], back1["wide="][0]]),
            sums[2 * LAYERS :],
        )

    return program


def solution(mesh):
    batch = P(AXES, None, None)
    columns = P(None, AXES)
    matrix = P(None, AXES, None)
    return jax.shard_map(
        build(mesh),
        mesh=mesh,
        in_specs=(
            batch,
            P(AXES, None),
            batch,
            columns,
            columns,
            matrix,
            matrix,
            matrix,
            columns,
            matrix,
            columns,
        ),
        out_specs=(
            batch,
            batch,
            columns,
            columns,
            matrix,
            matrix,
            matrix,
            columns,
            matrix,
            columns,
        ),
        check_vma=False,
    )
```

```python
import functools

import jax
import jax.numpy as jnp
from jax import lax
from jax.experimental import pallas as pl
from jax.experimental.pallas import tpu as pltpu
from jax.sharding import PartitionSpec as P

HEADS = 16
HEAD = 64
ROT = 32
LAYERS = 2
AXES = ("dp", "fsdp")

CORE_BIT = 0
PAIR_BIT = 2
FIRST_BIT = 3

layer_eps = 1e-05
gelu_scale = 0.7978845608028654
masked_fill = -1000000000.0
f32 = jnp.float32
bf16 = jnp.bfloat16


def gelu_and_slope(values):
    inner = jnp.tanh(gelu_scale * (values + 0.044715 * values * values * values))
    slope = 0.5 * (1.0 + inner) + 0.5 * values * (1.0 - inner * inner) * gelu_scale * (
        1.0 + 3.0 * 0.044715 * values * values
    )
    return 0.5 * values * (1.0 + inner), slope


def sequence_tables(segment_ids):
    length = segment_ids.shape[-1]
    index_grid = lax.broadcasted_iota(jnp.int32, segment_ids.shape, 1)
    before = segment_ids[:, None, :] < segment_ids[:, :, None]
    begin = jnp.sum(before, axis=-1, dtype=jnp.int32)
    lane = jnp.arange(2 * HEAD) % HEAD
    half_rot = ROT // 2
    frequency = 10000.0 ** (-((lane % half_rot).astype(f32) * 2.0 / ROT))
    frequency = jnp.where(lane < ROT, frequency, 0.0)
    angles = (index_grid - begin).astype(f32)[..., None] * frequency
    start = jnp.broadcast_to(begin.astype(f32)[..., None], segment_ids.shape + (2 * HEAD,))
    return jnp.concatenate([jnp.cos(angles), jnp.sin(angles), start], axis=-1).reshape(
        -1, 6 * HEAD
    )


def norm_stats(hidden):
    mean_value = jnp.mean(hidden, axis=-1, keepdims=True)
    centered = hidden - mean_value
    variance = jnp.mean(centered * centered, axis=-1, keepdims=True)
    scale = lax.rsqrt(variance + layer_eps)
    return centered * scale, scale


def turn(values, cosine, sine, sign):
    width = values.shape[1]
    half_rot = ROT // 2
    lane = lax.broadcasted_iota(jnp.int32, values.shape, 1) % HEAD
    ahead = pltpu.roll(values, width - half_rot, 1)
    behind = pltpu.roll(values, half_rot, 1)
    partner = jnp.where(lane < half_rot, -ahead, behind)
    return values * cosine + (sign * sine) * partner


def head_tables(table_ref, width):
    table = table_ref[...]
    copies = width // (2 * HEAD)
    cosine = jnp.concatenate([table[:, : 2 * HEAD]] * copies, axis=1)
    sine = jnp.concatenate([table[:, 2 * HEAD : 4 * HEAD]] * copies, axis=1)
    return cosine, sine, table[:, 4 * HEAD : 4 * HEAD + 1]


def visible(begin, length):
    row = lax.broadcasted_iota(jnp.int32, (length, length), 0)
    col = lax.broadcasted_iota(jnp.int32, (length, length), 1)
    return jnp.logical_and(col <= row, col.astype(f32) >= begin)


def only_head(values, head):
    lane = lax.broadcasted_iota(jnp.int32, values.shape, 1) // HEAD
    return jnp.where(lane == head, values, jnp.zeros_like(values))


def dot_last(left, right):
    return lax.dot_general(left, right, (((1,), (1,)), ((), ())), preferred_element_type=f32)


def dot_first(left, right):
    return lax.dot_general(left, right, (((0,), (0,)), ((), ())), preferred_element_type=f32)


def attend_kernel(normed_ref, weight_ref, table_ref, turned_ref, stats_ref, attended_ref):
    length = normed_ref.shape[0]
    width = attended_ref.shape[1]
    cosine, sine, begin = head_tables(table_ref, width)
    projected = jnp.dot(normed_ref[...], weight_ref[...], preferred_element_type=f32)
    query = turn(projected[:, :width], cosine, sine, 1.0).astype(bf16)
    key = turn(projected[:, width : 2 * width], cosine, sine, 1.0).astype(bf16)
    value = projected[:, 2 * width :].astype(bf16)
    turned_ref[:, :width] = query
    turned_ref[:, width : 2 * width] = key
    turned_ref[:, 2 * width :] = value
    seen = visible(begin, length)
    stats_lane = lax.broadcasted_iota(jnp.int32, stats_ref.shape, 1)
    stats = jnp.zeros(stats_ref.shape, f32)
    total = jnp.zeros((length, width), f32)
    for head in range(width // HEAD):
        scores = dot_last(only_head(query, head), key) * HEAD ** (-0.5)
        scores = jnp.where(seen, scores, masked_fill)
        row_max = jnp.max(scores, axis=1, keepdims=True)
        exponent = jnp.exp(scores - row_max)
        row_total = jnp.sum(exponent, axis=1, keepdims=True)
        probs = (exponent / row_total).astype(bf16)
        total += jnp.dot(probs, only_head(value, head), preferred_element_type=f32)
        stats = jnp.where(stats_lane == head, row_max, stats)
        stats = jnp.where(stats_lane == head + HEADS, row_total, stats)
    stats_ref[...] = stats
    attended_ref[...] = total.astype(bf16)


def activate_kernel(normed_ref, weight_ref, shift_ref, act_ref, slope_ref):
    pre = jnp.dot(normed_ref[...], weight_ref[...], preferred_element_type=f32) + shift_ref[...]
    act, slope = gelu_and_slope(pre)
    act_ref[...] = act.astype(bf16)
    slope_ref[...] = slope.astype(bf16)


def part_ways(value, kept_ref, away_ref):
    here = pl.program_id(0) < pl.num_programs(0) // 2

    @pl.when(here)
    def _():
        kept_ref[...] = value

    @pl.when(jnp.logical_not(here))
    def _():
        away_ref[...] = value.astype(bf16)


def leave_kernel(attended_ref, attn_back_ref, act_ref, mlp_back_ref, kept_ref, away_ref):
    value = jnp.dot(
        attended_ref[...], attn_back_ref[...], preferred_element_type=f32
    ) + jnp.dot(act_ref[...], mlp_back_ref[...], preferred_element_type=f32)
    part_ways(value, kept_ref, away_ref)


def deep_product_kernel(source_ref, left_ref, right_ref, own_ref, away_ref, whole_ref):
    whole_ref[...] = dot_first(left_ref[...], right_ref[...]).astype(bf16)
    chunks, rows, _ = own_ref.shape
    for at in range(chunks):
        for first, out_ref in ((0, own_ref), (chunks, away_ref)):
            begin = pl.multiple_of(source_ref[first + at] * rows, rows)
            out_ref[at] = whole_ref[pl.ds(begin, rows), :]


def wide_product_kernel(
    source_ref, act_ref, attended_ref, right_ref, own_ref, away_ref, units_ref, heads_ref
):
    units_ref[...] = dot_first(act_ref[...], right_ref[...]).astype(bf16)
    heads_ref[...] = dot_first(attended_ref[...], right_ref[...]).astype(bf16)
    blocks = own_ref.shape[0]
    units = units_ref.shape[0] // (2 * blocks)
    rows = heads_ref.shape[0] // (2 * blocks)
    for at in range(blocks):
        for first, out_ref in ((0, own_ref), (blocks, away_ref)):
            begin = pl.multiple_of(source_ref[first + at] * units, units)
            out_ref[at, :units] = units_ref[pl.ds(begin, units), :]
            begin = pl.multiple_of(source_ref[2 * blocks + first + at] * rows, rows)
            out_ref[at, units:] = heads_ref[pl.ds(begin, rows), :]


def product(kernel, source, lefts, right, shape, scratch):
    blocks, rows, width = shape
    tile = 256
    out = jax.ShapeDtypeStruct(shape, bf16)
    return pl.pallas_call(
        kernel,
        grid=(width // tile,),
        in_specs=[pl.BlockSpec(memory_space=pltpu.SMEM)]
        + [
            pl.BlockSpec(left.shape, lambda i: (0, 0), pipeline_mode=pl.Buffered(1))
            for left in lefts
        ]
        + [pl.BlockSpec((right.shape[0], tile), lambda i: (0, i))],
        out_specs=[pl.BlockSpec((blocks, rows, tile), lambda i: (0, 0, i))] * 2,
        out_shape=[out, out],
        scratch_shapes=[pltpu.VMEM((size, tile), bf16) for size in scratch],
        compiler_params=pltpu.CompilerParams(vmem_limit_bytes=40 << 20),
        cost_estimate=pl.CostEstimate(flops=0, bytes_accessed=1024, transcendentals=0),
    )(source, *lefts, right)


def back_kernel(
    grad_ref,
    attn_back_ref,
    mlp_back_ref,
    slope_ref,
    table_ref,
    turned_ref,
    stats_ref,
    attn_in_ref,
    mlp_in_ref,
    pre_ref,
    projected_ref,
    kept_ref,
    away_ref,
):
    length = grad_ref.shape[0]
    width = attn_back_ref.shape[0]
    cosine, sine, begin = head_tables(table_ref, width)
    d_act = dot_last(grad_ref[...], mlp_back_ref[...])
    d_pre = (d_act * slope_ref[...].astype(f32)).astype(bf16)
    pre_ref[...] = d_pre
    d_attended = dot_last(grad_ref[...], attn_back_ref[...]).astype(bf16)
    query = turned_ref[:, :width]
    key = turned_ref[:, width : 2 * width]
    value = turned_ref[:, 2 * width :]
    seen = visible(begin, length)
    stats = stats_ref[...]
    d_query = jnp.zeros((length, width), f32)
    d_key = jnp.zeros((length, width), f32)
    d_value = jnp.zeros((length, width), f32)
    for head in range(width // HEAD):
        query_head = only_head(query, head)
        scores = dot_last(query_head, key) * HEAD ** (-0.5)
        scores = jnp.where(seen, scores, masked_fill)
        row_max = stats[:, head : head + 1]
        row_total = stats[:, head + HEADS : head + HEADS + 1]
        probs = jnp.exp(scores - row_max) / row_total
        d_head = only_head(d_attended, head)
        d_value += dot_first(probs.astype(bf16), d_head)
        d_probs = dot_last(d_head, value)
        row_dot = jnp.sum(probs * d_probs, axis=1, keepdims=True)
        d_scores = (probs * (d_probs - row_dot)).astype(bf16)
        d_query += jnp.dot(d_scores, only_head(key, head), preferred_element_type=f32)
        d_key += dot_first(d_scores, query_head)
    projected_ref[:, :width] = turn(d_query * HEAD ** (-0.5), cosine, sine, -1.0).astype(bf16)
    projected_ref[:, width : 2 * width] = turn(
        d_key * HEAD ** (-0.5), cosine, sine, -1.0
    ).astype(bf16)
    projected_ref[:, 2 * width :] = d_value.astype(bf16)
    value = dot_last(projected_ref[...], attn_in_ref[...]) + dot_last(d_pre, mlp_in_ref[...])
    part_ways(value, kept_ref, away_ref)


def by_sequence(kernel, length, operands, whole, results):
    count = operands[0].shape[0] // length

    def spec(value):
        if value.shape[0] == count * length:
            return pl.BlockSpec((length, value.shape[1]), lambda i: (i, 0))
        if value.dtype == f32:
            return pl.BlockSpec((length, value.shape[1]), lambda i: (jnp.minimum(i, 1), 0))
        return pl.BlockSpec((length, value.shape[1]), lambda i: (jnp.maximum(i - 2, 0), 0))

    return pl.pallas_call(
        kernel,
        grid=(count,),
        in_specs=[
            pl.BlockSpec(value.shape, lambda i: (0, 0), pipeline_mode=pl.Buffered(1))
            if at in whole
            else pl.BlockSpec((length, value.shape[1]), lambda i: (i, 0))
            for at, value in enumerate(operands)
        ],
        out_specs=[spec(value) for value in results],
        out_shape=results,
        compiler_params=pltpu.CompilerParams(vmem_limit_bytes=48 << 20),
        cost_estimate=pl.CostEstimate(flops=0, bytes_accessed=1024, transcendentals=0),
    )(*operands)


def place_kernel(cuts, same, where_ref, *refs):
    pieces, outs = refs[: -len(cuts)], refs[-len(cuts) :]
    at = 0
    for (top, bottom, left, right), out_ref in zip(cuts, outs):
        at = 0 if same else at
        for piece_ref in pieces:
            for block in range(piece_ref.shape[0]):
                out_ref[pl.ds(where_ref[at], 1)] = piece_ref[
                    pl.ds(block, 1), pl.ds(top, bottom - top), pl.ds(left, right - left)
                ]
                at += 1


def place(pieces, where, cuts, same=False):
    blocks = sum(piece.shape[0] for piece in pieces)
    placed = pl.pallas_call(
        functools.partial(place_kernel, cuts, same),
        in_specs=[pl.BlockSpec(memory_space=pltpu.SMEM)]
        + [pl.BlockSpec(memory_space=pltpu.VMEM)] * len(pieces),
        out_specs=[pl.BlockSpec(memory_space=pltpu.VMEM)] * len(cuts),
        out_shape=[
            jax.ShapeDtypeStruct((blocks, bottom - top, right - left), pieces[0].dtype)
            for top, bottom, left, right in cuts
        ],
        compiler_params=pltpu.CompilerParams(vmem_limit_bytes=40 << 20),
        cost_estimate=pl.CostEstimate(flops=0, bytes_accessed=1024, transcendentals=0),
    )(where, *pieces)
    return [value.reshape(-1, value.shape[-1]) for value in placed]


def build(mesh):
    count = mesh.shape["dp"] * mesh.shape["fsdp"]
    bits = count.bit_length() - 1
    head_bits = HEADS.bit_length() - 1
    every = list(range(bits - 1, -1, -1))
    shared = [b for b in every if b not in (CORE_BIT, PAIR_BIT)]
    others = [b for b in shared if b != FIRST_BIT]
    steps = len(others)
    crossing = [
        [
            (i, i ^ (1 << (others[::-1] if (i >> CORE_BIT) & 1 else others)[step]))
            for i in range(count)
        ]
        for step in range(steps)
    ]
    unit_bits = others[::-1] + [FIRST_BIT]
    stands = list(range(bits))
    for share_bit, head_bit in ((PAIR_BIT, 1), (CORE_BIT, 3)):
        target = bits - head_bits + head_bit
        if target != share_bit:
            stands[share_bit], stands[target] = target, share_bit
    exchange = [
        (i, sum(((i >> stands[b]) & 1) << b for b in range(bits))) for i in range(count)
    ]
    head_order = [stands[b] for b in every if stands[b] not in (CORE_BIT, PAIR_BIT)]

    def program(
        tokens, segment_ids, cotangent, ln_gain, ln_bias, w_qkv, w_out, w_in, b_in, w_fo, b_fo
    ):
        device = lax.axis_index(AXES)
        seq_len, width = tokens.shape[1:]
        rows = w_qkv.shape[1]
        units = w_fo.shape[1]
        share_units = units * count // 4
        share_width = width // 4
        history = {}
        at_once = [3, 1]
        operand = [None]

        def pin(value, *earlier):
            return lax.optimization_barrier((value,) + earlier)[0]

        def gated(gate, value):
            return value if gate is None else pin(value, *gate)

        def flag(b):
            return (device >> b) & 1

        def send(value, way):
            pairs = way if isinstance(way, list) else [(i, i ^ (1 << way)) for i in range(count)]
            return lax.ppermute(value, AXES, pairs)

        def half(value, axis, own, b):
            return lax.dynamic_index_in_dim(
                value, flag(b) if own else 1 - flag(b), axis, keepdims=False
            )

        def pair_up(mine, other, b):
            high = flag(b) == 1
            return jnp.stack([jnp.where(high, other, mine), jnp.where(high, mine, other)])

        def arrange(value, have, want):
            rest = list(range(len(have), value.ndim))
            return value.transpose([have.index(b) for b in want] + rest)

        def position(order, mask):
            other = device ^ mask
            place_of = 0
            for b in order:
                place_of = 2 * place_of + ((other >> b) & 1)
            return place_of

        def cross(value, way):
            past = history.setdefault("first" if way == FIRST_BIT else "others", [])
            depth = at_once[way == FIRST_BIT]
            if len(past) >= depth:
                value = pin(value, past[-depth])
            operand[0] = value
            arrived = send(value, way)
            past.append(arrived)
            return arrived

        odd = flag(CORE_BIT) == 1

        def step_mask(step):
            return jnp.where(odd, 1 << others[::-1][step], 1 << others[step])

        def masks(found, order):
            for mask in order:
                found = found + [m | mask for m in found]
            return found

        gather_masks = [1 << FIRST_BIT] + [step_mask(step) for step in range(steps)]
        share_masks = masks([0], [1 << CORE_BIT, 1 << PAIR_BIT])

        def gather(value):
            for at, way in enumerate([FIRST_BIT] + crossing):
                arrived = cross(value, way)
                if at == steps:
                    yield [value, arrived]
                else:
                    arrived = gated((yield arrived), arrived)
                    value = jnp.concatenate([value, arrived])

        def scatter(own, away):
            arrived = cross(away, crossing[-1])
            for way in crossing[-2::-1] + [FIRST_BIT]:
                arrived = gated((yield arrived), arrived)
                value = (own.astype(f32) + arrived.astype(f32)).astype(bf16)
                middle = value.shape[0] // 2
                own = value[:middle]
                arrived = cross(value[middle:], way)
            arrived = gated((yield arrived), arrived)
            return own[0].astype(f32) + arrived[0].astype(f32)

        def spread(value):
            pair = jnp.concatenate([value, send(value, PAIR_BIT)])
            return jnp.concatenate([pair, send(pair, CORE_BIT)])

        def collect_core(kept, away):
            kept = (kept + send(away, CORE_BIT).astype(f32)).reshape(2, seq_len, width)
            return kept[0], kept[1].astype(bf16)

        def qkv_columns(value):
            parts = value.reshape(rows, 3, 2, 2, 2, 2 * HEAD)
            return parts.transpose(2, 4, 0, 1, 3, 5).reshape(2, 2, rows, 3 * share_width)

        def unit_columns(value):
            parts = value.reshape([rows] + [2] * bits + [units])
            where = {b: 1 + i for i, b in enumerate(every)}
            order = [where[CORE_BIT], where[PAIR_BIT], 0] + [where[b] for b in unit_bits]
            return parts.transpose(order + [bits + 1]).reshape(2, 2, rows, share_units)

        def reach(attn_part, mlp_part):
            columns = jnp.concatenate([qkv_columns(attn_part), unit_columns(mlp_part)], axis=-1)
            mine = half(columns, 0, True, CORE_BIT)
            arrived = send(half(columns, 0, False, CORE_BIT), CORE_BIT)
            columns = jnp.stack([mine, arrived], axis=1)
            mine = half(columns, 0, True, PAIR_BIT)
            arrived = send(half(columns, 0, False, PAIR_BIT), PAIR_BIT)
            return jnp.concatenate([mine, arrived])

        every_mask = masks([0], gather_masks)
        deep_where = jnp.stack(
            [position(every, outer | inner) for outer in every_mask for inner in share_masks]
        )
        wide_where = jnp.stack(
            [position(unit_bits, m) for m in every_mask]
            + [position(head_order, m) for m in every_mask]
        )

        def like(columns, kind):
            return jax.ShapeDtypeStruct((4 * seq_len, columns), kind)

        def advance(chains, names, *gate):
            for name in names:
                chains[name + "#"] = chains.get(name + "#", 0) + 1
                held = gate if gate and chains[name + "#"] > 1 else None
                try:
                    chains[name + "="] = chains[name].send(held)
                    chains[name + "<"] = operand[0]
                except StopIteration:
                    pass

        def finish(chains, name):
            while chains.get(name + "#", 0) < 1 + steps:
                advance(chains, [name])
            return chains[name + "="]

        def finish_deep(chains, name):
            pieces = finish(chains, name)
            return place(pieces, deep_where, ((0, rows, 0, pieces[0].shape[-1]),))[0]

        def finish_wide(chains):
            return place(
                finish(chains, "wide"),
                wide_where,
                ((0, units, 0, width), (units, units + rows, 0, width)),
            )

        def enter(hidden, depth):
            centered, _ = norm_stats(hidden)
            return spread((centered * gains[depth] + shifts[depth]).astype(bf16))

        def attend(normed, attn_in):
            return by_sequence(
                attend_kernel,
                seq_len,
                (normed, attn_in, tables),
                (1,),
                [like(3 * share_width, bf16), like(2 * HEAD, f32), like(share_width, bf16)],
            )

        def activate(normed, mlp_in, depth):
            return by_sequence(
                activate_kernel,
                seq_len,
                (normed, mlp_in, unit_shifts[depth][None]),
                (1, 2),
                [like(share_units, bf16), like(share_units, bf16)],
            )

        def ways():
            half_length = 2 * seq_len
            return [
                jax.ShapeDtypeStruct((half_length, width), f32),
                jax.ShapeDtypeStruct((half_length, width), bf16),
            ]

        def leave(attended, attn_back, act, mlp_back):
            return by_sequence(
                leave_kernel, seq_len, (attended, attn_back, act, mlp_back), (1, 3), ways()
            )

        def deep_product(left, right):
            keep = sum(1 << b for b in shared)
            source = jnp.stack(
                [
                    ((device ^ mask) & keep) | (pair << PAIR_BIT) | (core << CORE_BIT)
                    for mask in every_mask
                    for pair in range(2)
                    for core in range(2)
                ]
            )
            shape = (count // 2, rows, right.shape[1])
            if rows % 16:
                chunks = dot_first(left, right).astype(bf16).reshape(count, rows, -1)[source]
                own, away = chunks[: count // 2], chunks[count // 2 :]
            else:
                own, away = product(deep_product_kernel, source, (left,), right, shape, (width,))
            return [value.reshape(count // 8, 4 * rows, -1) for value in (own, away)]

        def scatter_deep(left, right):
            value = yield from scatter(*deep_product(left, right))
            value = value.astype(bf16).reshape(2, 2, rows, -1)
            arrived = send(half(value, 0, False, PAIR_BIT), PAIR_BIT)
            value = pair_up(half(value, 0, True, PAIR_BIT), arrived, PAIR_BIT)
            arrived = send(half(value, 1, False, CORE_BIT), CORE_BIT)
            yield pair_up(half(value, 1, True, CORE_BIT), arrived, CORE_BIT).astype(f32)

        def restore_qkv(value):
            parts = value.reshape(2, 2, rows, 3, 2, 2 * HEAD)
            return parts.transpose(2, 3, 0, 4, 1, 5).reshape(rows, 3 * width)

        def restore_units(value):
            parts = value.reshape([2, 2, rows] + [2] * len(unit_bits) + [units])
            where = {b: 3 + i for i, b in enumerate(unit_bits)}
            where[CORE_BIT], where[PAIR_BIT] = 0, 1
            order = [2] + [where[b] for b in every] + [parts.ndim - 1]
            return parts.transpose(order).reshape(rows, units * count)

        def wide_product(act, attended, grad_low):
            blocks = count // 4
            source = jnp.stack(
                [position(unit_bits, m) for m in every_mask]
                + [position(head_order, m) for m in every_mask]
            )
            shape = (blocks // 2, units + rows, width)
            if rows % 16:
                units_part = dot_first(act, grad_low).astype(bf16).reshape(blocks, units, width)
                heads_part = dot_first(attended, grad_low).astype(bf16).reshape(blocks, rows, width)
                value = jnp.concatenate(
                    [units_part[source[:blocks]], heads_part[source[blocks:]]], axis=1
                )
                return value[: blocks // 2], value[blocks // 2 :]
            return product(
                wide_product_kernel,
                source,
                (act, attended),
                grad_low,
                shape,
                (share_units, share_width),
            )

        def scatter_wide(act, attended, grad_low):
            value = yield from scatter(*wide_product(act, attended, grad_low))
            rows_out = send(value[units:].astype(bf16), exchange)
            yield value[:units], rows_out.astype(f32)

        def norm_all(hidden, depth):
            centered, _ = norm_stats(hidden)
            return (centered * gains[depth] + shifts[depth]).astype(bf16)

        def small_lanes():
            lane = lax.broadcasted_iota(jnp.int32, (rows, width), 1)
            spot = lax.broadcasted_iota(jnp.int32, (rows, width), 0)
            into_width = (lane == device * rows + spot).astype(bf16)
            lane = lax.broadcasted_iota(jnp.int32, (units, share_units), 1)
            spot = lax.broadcasted_iota(jnp.int32, (units, share_units), 0)
            into_units = (lane == position(unit_bits, 0) * units + spot).astype(bf16)
            thin = jnp.dot(
                jnp.concatenate([ln_gain, ln_bias, b_fo]),
                into_width,
                preferred_element_type=f32,
            )
            thick = jnp.dot(b_in, into_units, preferred_element_type=f32)
            return jnp.concatenate([thin.reshape(-1, 128), thick.reshape(-1, 128)]).astype(bf16)

        blocks0 = reach(w_qkv[0], w_in[0])
        small = small_lanes()
        cut = 3 * LAYERS * width // 128
        thin, thick = small[:cut], small[cut:]
        for b in (CORE_BIT, PAIR_BIT):
            thin = thin + send(thin, b)
        small = jnp.concatenate([thin, thick])
        first = {
            "qkv": gather(blocks0[:, :, : 3 * share_width]),
            "in": gather(blocks0[:, :, 3 * share_width :]),
        }
        advance(first, ["qkv"])
        qkv_arrived = first["qkv="]
        outs = send(w_out, exchange)
        first["wide"] = gather(jnp.concatenate([w_fo[0], outs[0]])[None])
        ids = spread(pin(segment_ids.astype(bf16), first["qkv<"])).astype(jnp.int32)
        tokens_all = spread(pin(tokens[0], ids))
        small = pin(small, first["qkv<"])
        small = small + send(small, FIRST_BIT)
        advance(first, ["in", "qkv"])
        small = pin(small, first["qkv<"])
        for b in others:
            small = small + send(small, b)
        blocks1 = reach(pin(w_qkv[1], first["qkv<"]), pin(w_in[1], first["qkv<"]))
        second = {
            "deep": gather(blocks1),
            "wide": gather(jnp.concatenate([w_fo[1], outs[1]])[None]),
        }
        advance(first, ["qkv"])
        tables = sequence_tables(pin(ids, first["qkv<"]))
        unit_shifts = small[cut:].reshape(LAYERS, share_units).astype(f32)
        small = small[:cut]
        small = small.reshape(3, LAYERS, width).astype(f32)
        gains, shifts, out_shifts = small[0], small[1], small[2]
        grad_low1 = spread(pin(cotangent[0], first["in="]))
        advance(first, ["in", "wide"])
        advance(first, ["in"])
        advance(first, ["wide"], blocks1)
        advance(second, ["deep"])
        hidden0 = tokens[0].astype(f32)
        normed0 = norm_all(
            pin(tokens_all, first["in<"], first["wide<"], second["deep<"]).astype(f32), 0
        )
        attn_in0 = finish_deep(first, "qkv")
        turned0, stats0, attended0 = attend(normed0, attn_in0)
        advance(first, ["wide"], attended0)
        advance(second, ["deep"], attended0)
        advance(second, ["wide"])
        mlp_in0 = finish_deep(first, "in")
        act0, slope0 = activate(
            pin(normed0, first["wide<"], second["deep<"], second["wide<"]), mlp_in0, 0
        )
        advance(second, ["deep"], act0)
        mlp_back0, attn_back0 = finish_wide(first)
        kept0, away0 = leave(pin(attended0, second["deep<"]), attn_back0, act0, mlp_back0)
        kept0, over0 = collect_core(kept0, pin(away0, second["wide="]))
        arrived0 = send(over0, PAIR_BIT)
        advance(second, ["wide"], over0)
        hidden1 = (
            hidden0 + kept0 + pin(arrived0, second["wide<"]).astype(f32) + out_shifts[0]
        )
        centered1, _ = norm_stats(hidden1)
        normed1 = (centered1 * gains[1] + shifts[1]).astype(bf16)
        other1 = send(normed1, PAIR_BIT)
        advance(second, ["wide"], normed1)
        pair1 = jnp.concatenate([normed1, pin(other1, second["wide<"])])
        normed1 = jnp.concatenate([pair1, send(pair1, CORE_BIT)])
        attn_in1, mlp_in1 = place(
            finish(second, "deep"),
            deep_where,
            ((0, rows, 0, 3 * share_width), (0, rows, 3 * share_width, 3 * share_width + share_units)),
            True,
        )
        turned1, stats1, attended1 = attend(normed1, attn_in1)
        act1, slope1 = activate(normed1, mlp_in1, 1)
        mlp_back1, attn_back1 = finish_wide(second)

        def back(grad_low, attn_back, mlp_back, slope, turned, stats, attn_in, mlp_in):
            return by_sequence(
                back_kernel,
                seq_len,
                (grad_low, attn_back, mlp_back, slope, tables, turned, stats, attn_in, mlp_in),
                (1, 2, 7, 8),
                [like(share_units, bf16), like(3 * share_width, bf16)] + ways(),
            )

        def norm_back(hidden, grad, d_normed, depth):
            centered, scale = norm_stats(hidden)
            d_gain = jnp.sum(d_normed * centered, axis=0)
            d_shift = jnp.sum(d_normed, axis=0)
            d_centered = d_normed * gains[depth]
            grad = grad + scale * (
                d_centered
                - jnp.mean(d_centered, axis=-1, keepdims=True)
                - centered * jnp.mean(d_centered * centered, axis=-1, keepdims=True)
            )
            return grad, d_gain, d_shift

        def column_sum(value):
            return jnp.sum(value, axis=0, dtype=f32)

        at_once[:] = 9, 9
        grad1 = cotangent[0].astype(f32)
        d_shift_out1 = column_sum(cotangent[0])
        back1 = {"wide": scatter_wide(act1, attended1, grad_low1)}
        advance(back1, ["wide"])
        d_pre1, d_projected1, kept1, away1 = back(
            pin(grad_low1, back1["wide<"]),
            attn_back1,
            mlp_back1,
            slope1,
            turned1,
            stats1,
            attn_in1,
            mlp_in1,
        )
        away1 = pin(away1, back1["wide="])
        kept1, over1 = collect_core(kept1, away1)
        arrived1 = send(over1, PAIR_BIT)
        advance(back1, ["wide"], away1)
        back1["in"] = scatter_deep(normed1, pin(d_pre1, over1, back1["wide<"]))
        advance(back1, ["in"])
        back1["qkv"] = scatter_deep(normed1, pin(d_projected1, back1["in<"]))
        advance(back1, ["qkv"])
        advance(back1, ["wide"], back1["in<"])
        d_normed1 = kept1 + pin(arrived1, back1["wide<"], back1["qkv<"]).astype(f32)
        grad0, d_gain1, d_shift1 = norm_back(hidden1, grad1, d_normed1, 1)
        own_low0 = grad0.astype(bf16)
        other_low0 = send(own_low0, PAIR_BIT)
        advance(back1, ["in", "qkv"], own_low0)
        pair_low0 = jnp.concatenate(
            [own_low0, pin(other_low0, back1["in="], back1["qkv<"], back1["wide="])]
        )
        grad_low0 = jnp.concatenate([pair_low0, send(pair_low0, CORE_BIT)])
        advance(back1, ["in"], other_low0)
        back0 = {"wide": scatter_wide(act0, attended0, grad_low0)}
        advance(back0, ["wide"])
        d_pre0, d_projected0, kept0, away0 = back(
            pin(grad_low0, back0["wide<"], back1["in<"]),
            attn_back0,
            mlp_back0,
            slope0,
            turned0,
            stats0,
            attn_in0,
            mlp_in0,
        )
        away0 = pin(away0, back0["wide="], back1["in="], back1["qkv="])
        kept0, over0 = collect_core(kept0, away0)
        arrived0 = send(over0, PAIR_BIT)
        advance(back0, ["wide"], away0)
        advance(back1, ["qkv"], over0)
        back0["in"] = scatter_deep(
            normed0, pin(d_pre0, over0, back0["wide<"], back1["qkv<"])
        )
        advance(back0, ["in"])
        back0["qkv"] = scatter_deep(normed0, pin(d_projected0, back0["in<"]))
        advance(back0, ["qkv"])
        advance(back0, ["wide"], back0["in<"])
        advance(back1, ["in", "qkv"], back0["qkv<"])
        kept, away = leave(pin(attended1, back0["qkv<"], arrived0), attn_back1, act1, mlp_back1)
        kept, over = collect_core(kept, away)
        last = send(over, PAIR_BIT)
        advance(back0, ["in", "qkv"], over)
        d_normed0 = kept0 + pin(
            arrived0, back0["wide<"], back0["in<"], back0["qkv<"]
        ).astype(f32)
        d_tokens, d_gain0, d_shift0 = norm_back(hidden0, grad0, d_normed0, 0)
        advance(back0, ["in", "qkv"])
        late = back0["in<"], back0["wide<"]
        d_units1 = column_sum(pin(d_pre1, *late))
        d_units0 = column_sum(pin(d_pre0, *late))
        d_shift_out0 = column_sum(pin(own_low0, *late))
        advance(back1, ["wide"], *late)
        layer_out = hidden1 + kept + pin(last, *late).astype(f32)
        layer_out = (layer_out + out_shifts[1]).astype(bf16)
        advance(back0, ["wide"], *late)
        for _ in range(bits):
            advance(back0, ["in", "qkv", "wide"])
            advance(back1, ["wide", "in", "qkv"])

        thin = jnp.stack([d_gain0, d_gain1, d_shift0, d_shift1, d_shift_out0, d_shift_out1])
        sums = jnp.concatenate(
            [thin.reshape(-1, 128), jnp.stack([d_units0, d_units1]).reshape(-1, 128)]
        )
        sums = pin(sums, *late)
        for b in [FIRST_BIT] + others:
            sums = sums + send(sums, b)
        d_units = sums[cut:].reshape(LAYERS, share_units)
        sums = sums[:cut]
        for b in (CORE_BIT, PAIR_BIT):
            sums = sums + send(sums, b)
        sums = sums.reshape(3 * LAYERS, width)
        sums = lax.dynamic_slice_in_dim(sums, device * rows, rows, 1)
        d_b_in = lax.dynamic_slice_in_dim(d_units, position(unit_bits, 0) * units, units, 1)
        return (
            layer_out[None],
            d_tokens[None],
            sums[:LAYERS],
            sums[LAYERS : 2 * LAYERS],
            jnp.stack([restore_qkv(back0["qkv="]), restore_qkv(back1["qkv="])]),
            jnp.stack([back0["wide="][1], back1["wide="][1]]),
            jnp.stack([restore_units(back0["in="]), restore_units(back1["in="])]),
            d_b_in,
            jnp.stack([back0["wide="][0], back1["wide="][0]]),
            sums[2 * LAYERS :],
        )

    return program


def solution(mesh):
    batch = P(AXES, None, None)
    columns = P(None, AXES)
    matrix = P(None, AXES, None)
    return jax.shard_map(
        build(mesh),
        mesh=mesh,
        in_specs=(
            batch,
            P(AXES, None),
            batch,
            columns,
            columns,
            matrix,
            matrix,
            matrix,
            columns,
            matrix,
            columns,
        ),
        out_specs=(
            batch,
            batch,
            columns,
            columns,
            matrix,
            matrix,
            matrix,
            columns,
            matrix,
            columns,
        ),
        check_vma=False,
    )
```
